32 devices in a mesh: dp: 2 (over core), ctx: 4 (over y, x), tp: 4 (over z).
Axes of the slice: x: 2, y: 2, z: 4, core: 2. Of those that a mesh axis runs over, the one named last changes fastest.
Arguments:
- hidden_in: bfloat16 [2, 1024, 768], P('dp', 'ctx'), may hold values from -6 to 6
- span_order: int32 [2, 8], P('dp'), may hold values from 0 to 7, each once within a row
- norm_gains: float32 [2, 768], replicated, may hold values from 0.5 to 1.5
- norm_biases: float32 [2, 768], replicated, may hold values from -1.75 to 1.75
- w_qkv: bfloat16 [768, 2304], P(('dp', 'ctx'), 'tp')
- qv_bias: float32 [1536], P('tp'), may hold values from -3 to 3
- w_dense: bfloat16 [768, 768], P(('dp', 'ctx'), 'tp'), may hold values from -0.875 to 0.875
- w_up: bfloat16 [768, 3072], P(('dp', 'ctx'), 'tp'), may hold values from -0.21875 to 0.21875
- up_bias: float32 [3072], P('tp'), may hold values from -3 to 3
- w_down: bfloat16 [768, 3072], P(('dp', 'ctx'), 'tp'), may hold values from -0.109375 to 0.109375
- out_bias: float32 [768], replicated, may hold values from -3 to 3
- grad_out: bfloat16 [2, 1024, 768], P('dp', 'ctx'), may hold values from -6 to 6
Outputs:
- layer_out: bfloat16 [2, 1024, 768], P('dp', 'ctx')
- grad_in: bfloat16 [2, 1024, 768], P('dp', 'ctx')
- grad_norm_gains: float32 [2, 768], replicated
- grad_norm_biases: float32 [2, 768], replicated
- grad_qkv: float32 [768, 2304], P(('dp', 'ctx'), 'tp')
- grad_qv_bias: float32 [1536], P('tp')
- grad_dense: float32 [768, 768], P(('dp', 'ctx'), 'tp')
- grad_up: float32 [768, 3072], P(('dp', 'ctx'), 'tp')
- grad_up_bias: float32 [3072], P('tp')
- grad_down: float32 [768, 3072], P(('dp', 'ctx'), 'tp')
- grad_out_bias: float32 [768], replicated
The draws below stay inside these ranges and needn't reach their ends.
Inputs may be any that keep to these rules, and one draw needn't show every extreme that they name: `span_order`: each row lists every block index once.
All inputs are finite; a program needn't handle non-finite values.
Results may differ from the reference program's by a relative error of at most 0.0084.
Values may be sent and summed in bfloat16 or wider, within the bound.
A program may use at most 128 MiB of HBM per device.

```python
import math
import jax
import jax.numpy as jnp
from jax import lax

D = 768
H = 12
HD = 64
FF = 3072
ROT = 16
SPAN = 128
SPANS = 8
SEQ = 1024
SEQS = 2


def draw_w_qkv(key, part):
    weights_all = jnp.clip(jax.random.normal(key, (D, H, 3, HD), jnp.float32), -4.0, 4.0) * (1.0 / math.sqrt(D))
    return weights_all.reshape(D, H * 3 * HD).astype(jnp.bfloat16)


def level_of(rng, dims, shards, smallest, largest):
    def one(dim, blocks):
        heights = jax.random.uniform(jax.random.fold_in(jax.random.fold_in(rng, 6), dim), (blocks,), jnp.float32, smallest / len(shards), largest / len(shards))
        return jnp.repeat(jnp.exp(heights), dims[dim] // blocks).reshape((-1,) + (1,) * (len(dims) - dim - 1))

    factor_of = one(*shards[0])
    for cut in shards[1:]:
        factor_of = factor_of * one(*cut)
    return factor_of


def centred(stream_key, extent, spread, bound, split=(), kind=jnp.bfloat16):
    factor_of = level_of(stream_key, extent, split, -0.22, 0.18) if split else 1.0
    result = jax.random.normal(stream_key, extent, jnp.float32) * spread * factor_of
    return jnp.minimum(jnp.maximum(result, -bound), bound).astype(kind)


def setup_inputs(seed: int = 0) -> dict:
    splits = jax.random.split(jax.random.key(seed), 13)
    return {
        "hidden_in": centred(splits[0], (SEQS, SEQ, D), 1.0, 6.0, ((0, 2), (1, 4))),
        "span_order": jax.vmap(lambda own: jax.random.permutation(own, SPANS))(jax.random.split(splits[1], SEQS)).reshape((SEQS, SPANS)).astype(jnp.int32),
        "norm_gains": jnp.clip(1.0 + 0.1 * jax.random.normal(splits[2], (2, D), jnp.float32), 0.5, 1.5),
        "norm_biases": centred(splits[3], (2, D), 0.3, 1.75, (), jnp.float32),
        "w_qkv": draw_w_qkv(jax.random.fold_in(splits[12], 71), 0),
        "qv_bias": centred(splits[5], (H * 2 * HD,), 0.5, 3.0, ((0, 4),), jnp.float32),
        "w_dense": centred(splits[6], (D, H * HD), (H * HD // 16) ** -0.5, 0.875, ((0, 8), (1, 4))),
        "w_up": centred(splits[7], (D, FF), D ** -0.5, 0.21875, ((0, 8), (1, 4))),
        "up_bias": centred(splits[8], (FF,), 0.5, 3.0, ((0, 4),), jnp.float32),
        "w_down": centred(splits[9], (D, FF), FF ** -0.5, 0.109375, ((0, 8), (1, 4))),
        "out_bias": centred(splits[10], (D,), 0.5, 3.0, (), jnp.float32),
        "grad_out": centred(splits[11], (SEQS, SEQ, D), 1.0, 6.0, ((0, 2), (1, 4))),
    }


EPS = 1e-05
NEG = -1e+30

def rounded(values):
    return lax.optimization_barrier(values.astype(jnp.bfloat16)).astype(jnp.float32)

def layer_norm(values, gain_vec, shift_vec):
    row_mean = lax.optimization_barrier(jnp.mean(values, axis=-1, keepdims=True))
    centered = values - row_mean
    variance = lax.optimization_barrier(jnp.mean(centered * centered, axis=-1, keepdims=True))
    inv_std = lax.rsqrt(variance + EPS)
    normed = centered * inv_std
    return (normed * gain_vec + shift_vec, normed, inv_std)

def norm_back(grad_normed, normed, inv_std, gain_vec):
    scaled = grad_normed * gain_vec
    return inv_std * (scaled - lax.optimization_barrier(jnp.mean(scaled, axis=-1, keepdims=True)) - normed * lax.optimization_barrier(jnp.mean(scaled * normed, axis=-1, keepdims=True)))

def rotary_tables(positions, rot_dims):
    half_rot = rot_dims // 2
    frequency = 1.0 / 10000.0 ** (jnp.arange(half_rot, dtype=jnp.float32) * (2.0 / rot_dims))
    angles = positions.astype(jnp.float32)[:, None] * frequency[None, :]
    return (jnp.cos(angles), jnp.sin(angles))

def rotate(vectors, cos_table, sin_table, rot_dims):
    half_rot = rot_dims // 2
    front_half = vectors[..., :half_rot]
    back_half = vectors[..., half_rot:rot_dims]
    cos_row = cos_table[:, None, :]
    sin_row = sin_table[:, None, :]
    return jnp.concatenate([front_half * cos_row - back_half * sin_row, back_half * cos_row + front_half * sin_row, vectors[..., rot_dims:]], axis=-1)

def gelu_value(hidden):
    return 0.5 * hidden * (1.0 + jax.scipy.special.erf(hidden * (1.0 / math.sqrt(2.0))))

def gelu_slope(hidden):
    return 0.5 * (1.0 + jax.scipy.special.erf(hidden * (1.0 / math.sqrt(2.0)))) + hidden * jnp.exp(-0.5 * hidden * hidden) * (1.0 / math.sqrt(2.0 * math.pi))

def reference(hidden_in, span_order, norm_gains, norm_biases, w_qkv, qv_bias, w_dense, w_up, up_bias, w_down, out_bias, grad_out):
    highest = lax.Precision.HIGHEST
    score_scale = 1.0 / math.sqrt(HD)
    query_rows = math.gcd(SEQ, 256)
    query_blocks = SEQ // query_rows
    bias_pair = qv_bias.reshape(H, 2, HD)

    def one_sequence(totals, packed):
        hidden_seq, order_seq, cot_seq = packed
        positions = (order_seq[:, None] * SPAN + jnp.arange(SPAN, dtype=jnp.int32)[None, :]).reshape(-1)
        inputs = hidden_seq.astype(jnp.float32)
        normed_one, hat_one, inv_one = layer_norm(inputs, norm_gains[0], norm_biases[0])
        normed_two, hat_two, inv_two = layer_norm(inputs, norm_gains[1], norm_biases[1])
        attn_in = normed_one.astype(jnp.bfloat16)
        mlp_in = normed_two.astype(jnp.bfloat16)
        projected = jnp.dot(attn_in, w_qkv, preferred_element_type=jnp.float32).reshape(SEQ, H, 3, HD)
        cos_table, sin_table = rotary_tables(positions, ROT)
        queries = rotate(projected[:, :, 0] + bias_pair[:, 0], cos_table, sin_table, ROT).astype(jnp.bfloat16)
        keys_rot = rotate(projected[:, :, 1], cos_table, sin_table, ROT).astype(jnp.bfloat16)
        values_in = (projected[:, :, 2] + bias_pair[:, 1]).astype(jnp.bfloat16)
        keys_float = keys_rot.astype(jnp.float32)
        values_float = values_in.astype(jnp.float32)
        query_split = queries.reshape(query_blocks, query_rows, H, HD)
        pos_split = positions.reshape(query_blocks, query_rows)

        def attend_block(block_in):
            query_blk, query_pos = block_in
            scores = jnp.einsum('qhd,khd->hqk', query_blk.astype(jnp.float32), keys_float, precision=highest) * score_scale
            allowed = (positions[None, :] <= query_pos[:, None])[None]
            scores = jnp.where(allowed, scores, NEG)
            row_max = lax.optimization_barrier(jnp.max(scores, axis=-1))
            weights = jnp.where(allowed, jnp.exp(scores - row_max[..., None]), 0.0)
            row_total = lax.optimization_barrier(jnp.sum(weights, axis=-1))
            mixed = jnp.einsum('hqk,khd->hqd', rounded(weights), values_float, precision=highest) / row_total[..., None]
            return (jnp.transpose(mixed, (1, 0, 2)), row_max + jnp.log(row_total))
        mixed_split, lse_split = lax.map(attend_block, (query_split, pos_split))
        attn_out = mixed_split.reshape(SEQ, H * HD).astype(jnp.bfloat16)
        attn_part = jnp.dot(attn_out, w_dense.T, preferred_element_type=jnp.float32)
        hidden_pre = jnp.dot(mlp_in, w_up, preferred_element_type=jnp.float32) + up_bias
        activated = gelu_value(hidden_pre).astype(jnp.bfloat16)
        mlp_part = jnp.dot(activated, w_down.T, preferred_element_type=jnp.float32)
        layer_seq = (inputs + out_bias + (attn_part + mlp_part)).astype(jnp.bfloat16)
        cot_float = cot_seq.astype(jnp.float32)
        out_bias_grad = lax.optimization_barrier(jnp.sum(cot_float, axis=0))
        down_grad = jnp.dot(cot_seq.T, activated, preferred_element_type=jnp.float32)
        pre_grad = jnp.dot(cot_seq, w_down, preferred_element_type=jnp.float32) * gelu_slope(hidden_pre)
        up_bias_grad = lax.optimization_barrier(jnp.sum(pre_grad, axis=0))
        pre_grad_b = pre_grad.astype(jnp.bfloat16)
        up_grad = jnp.dot(mlp_in.T, pre_grad_b, preferred_element_type=jnp.float32)
        normed_two_grad = jnp.dot(pre_grad_b, w_up.T, preferred_element_type=jnp.float32)
        dense_grad = jnp.dot(cot_seq.T, attn_out, preferred_element_type=jnp.float32)
        out_grad = jnp.dot(cot_seq, w_dense, preferred_element_type=jnp.float32).astype(jnp.bfloat16).reshape(SEQ, H, HD)
        row_delta = lax.optimization_barrier(jnp.sum(out_grad.astype(jnp.float32) * attn_out.reshape(SEQ, H, HD).astype(jnp.float32), axis=-1)).T
        grad_split = out_grad.reshape(query_blocks, query_rows, H, HD)
        delta_split = jnp.transpose(row_delta.reshape(H, query_blocks, query_rows), (1, 0, 2))

        def back_block(state_in, block_in):
            key_acc, value_acc = state_in
            query_blk, query_pos, grad_blk, delta_blk, lse_blk = block_in
            query_float = query_blk.astype(jnp.float32)
            grad_float = grad_blk.astype(jnp.float32)
            scores = jnp.einsum('qhd,khd->hqk', query_float, keys_float, precision=highest) * score_scale
            allowed = (positions[None, :] <= query_pos[:, None])[None]
            prob_table = jnp.where(allowed, jnp.exp(jnp.where(allowed, scores, NEG) - lse_blk[..., None]), 0.0)
            prob_grad = jnp.einsum('qhd,khd->hqk', grad_float, values_float, precision=highest)
            score_grad = rounded(prob_table * (prob_grad - delta_blk[..., None]))
            query_grad = jnp.einsum('hqk,khd->qhd', score_grad, keys_float, precision=highest) * score_scale
            key_acc = key_acc + jnp.einsum('hqk,qhd->khd', score_grad, query_float, precision=highest) * score_scale
            value_acc = value_acc + jnp.einsum('hqk,qhd->khd', rounded(prob_table), grad_float, precision=highest)
            return ((key_acc, value_acc), query_grad)
        empty = jnp.zeros((SEQ, H, HD), jnp.float32)
        (key_grad, value_grad), query_split_grad = lax.scan(back_block, (empty, empty), (query_split, pos_split, grad_split, delta_split, lse_split))
        query_grad = query_split_grad.reshape(SEQ, H, HD)
        query_pre = rotate(query_grad, cos_table, -sin_table, ROT)
        key_pre = rotate(key_grad, cos_table, -sin_table, ROT)
        qv_grad = jnp.stack([lax.optimization_barrier(jnp.sum(query_pre, axis=0)), lax.optimization_barrier(jnp.sum(value_grad, axis=0))], axis=1).reshape(-1)
        proj_grad = jnp.stack([query_pre, key_pre, value_grad], axis=2).reshape(SEQ, H * 3 * HD).astype(jnp.bfloat16)
        qkv_grad = jnp.dot(attn_in.T, proj_grad, preferred_element_type=jnp.float32)
        normed_one_grad = jnp.dot(proj_grad, w_qkv.T, preferred_element_type=jnp.float32)
        gain_grad = jnp.stack([lax.optimization_barrier(jnp.sum(normed_one_grad * hat_one, axis=0)), lax.optimization_barrier(jnp.sum(normed_two_grad * hat_two, axis=0))])
        bias_grad = jnp.stack([lax.optimization_barrier(jnp.sum(normed_one_grad, axis=0)), lax.optimization_barrier(jnp.sum(normed_two_grad, axis=0))])
        input_seq = (cot_float + norm_back(normed_one_grad, hat_one, inv_one, norm_gains[0]) + norm_back(normed_two_grad, hat_two, inv_two, norm_gains[1])).astype(jnp.bfloat16)
        parts = (gain_grad, bias_grad, qkv_grad, qv_grad, dense_grad, up_grad, up_bias_grad, down_grad, out_bias_grad)
        totals = jax.tree.map(lambda older, newer: older + newer, totals, parts)
        return (totals, (layer_seq, input_seq))
    start_totals = (jnp.zeros((2, D), jnp.float32), jnp.zeros((2, D), jnp.float32), jnp.zeros((D, H * 3 * HD), jnp.float32), jnp.zeros((H * 2 * HD,), jnp.float32), jnp.zeros((D, H * HD), jnp.float32), jnp.zeros((D, FF), jnp.float32), jnp.zeros((FF,), jnp.float32), jnp.zeros((D, FF), jnp.float32), jnp.zeros((D,), jnp.float32))
    totals, (layer_out, grad_in) = lax.scan(one_sequence, start_totals, (hidden_in, span_order, grad_out))
    gains_total, biases_total, qkv_total, qv_total, dense_total, up_total, up_bias_total, down_total, out_bias_total = totals
    return (layer_out, grad_in, gains_total, biases_total, qkv_total, qv_total, dense_total, up_total, up_bias_total, down_total, out_bias_total)
```

```python
import functools
import math

import jax
import jax.numpy as jnp
from jax import lax
from jax.experimental import pallas as pl
from jax.experimental.pallas import tpu as pltpu
from jax.sharding import PartitionSpec as P

HD = 64
ROT = 16
SPAN = 128


EPS = 1e-05
NEG = -1e30


def layer_norm(values, gain_vec, shift_vec):
    row_mean = jnp.mean(values, axis=-1, keepdims=True)
    centered = values - row_mean
    variance = jnp.mean(centered * centered, axis=-1, keepdims=True)
    inv_std = lax.rsqrt(variance + EPS)
    normed = centered * inv_std
    return (normed * gain_vec + shift_vec, normed, inv_std)


def norm_back(grad_normed, normed, inv_std, gain_vec):
    scaled = grad_normed * gain_vec
    return inv_std * (
        scaled
        - jnp.mean(scaled, axis=-1, keepdims=True)
        - normed * jnp.mean(scaled * normed, axis=-1, keepdims=True)
    )


def rotary_tables(positions, rot_dims):
    half_rot = rot_dims // 2
    frequency = 1.0 / 10000.0 ** (jnp.arange(half_rot, dtype=jnp.float32) * (2.0 / rot_dims))
    angles = positions.astype(jnp.float32)[:, None] * frequency[None, :]
    return (jnp.cos(angles), jnp.sin(angles))


def rotate(vectors, cos_table, sin_table, rot_dims):
    half_rot = rot_dims // 2
    front_half = vectors[..., :half_rot]
    back_half = vectors[..., half_rot:rot_dims]
    cos_row = cos_table[:, None, :]
    sin_row = sin_table[:, None, :]
    return jnp.concatenate(
        [
            front_half * cos_row - back_half * sin_row,
            back_half * cos_row + front_half * sin_row,
            vectors[..., rot_dims:],
        ],
        axis=-1,
    )


def gelu_value(hidden):
    return 0.5 * hidden * (1.0 + jax.scipy.special.erf(hidden * (1.0 / math.sqrt(2.0))))


def gelu_slope(hidden):
    return 0.5 * (1.0 + jax.scipy.special.erf(hidden * (1.0 / math.sqrt(2.0)))) + hidden * jnp.exp(
        -0.5 * hidden * hidden
    ) * (1.0 / math.sqrt(2.0 * math.pi))


def on_device(
    hidden_in,
    span_order,
    norm_gains,
    norm_biases,
    w_qkv,
    qv_bias,
    w_dense,
    w_up,
    up_bias,
    w_down,
    out_bias,
    grad_out,
):
    tok_rows = hidden_in.shape[1]
    local_heads = qv_bias.shape[0] // (2 * HD)
    head_cols = local_heads * HD
    score_scale = 1.0 / math.sqrt(HD)
    positions = (
        span_order[0][:, None] * SPAN + jnp.arange(SPAN, dtype=jnp.int32)[None, :]
    ).reshape(-1)
    own_pos = lax.dynamic_slice_in_dim(positions, lax.axis_index("ctx") * tok_rows, tok_rows)
    full_qkv, full_dense, full_up, full_down = (
        lax.all_gather(w_qkv, ("dp", "ctx"), axis=0, tiled=True),
        lax.all_gather(w_dense, ("dp", "ctx"), axis=0, tiled=True),
        lax.all_gather(w_up, ("dp", "ctx"), axis=0, tiled=True),
        lax.all_gather(w_down, ("dp", "ctx"), axis=0, tiled=True),
    )
    inputs = hidden_in[0].astype(jnp.float32)
    normed_one, hat_one, inv_one = layer_norm(inputs, norm_gains[0], norm_biases[0])
    normed_two, hat_two, inv_two = layer_norm(inputs, norm_gains[1], norm_biases[1])
    attn_in = normed_one.astype(jnp.bfloat16)
    mlp_in = normed_two.astype(jnp.bfloat16)
    projected = jnp.dot(attn_in, full_qkv, preferred_element_type=jnp.float32).reshape(
        tok_rows, local_heads, 3, HD
    )
    bias_pair = qv_bias.reshape(local_heads, 2, HD)
    cos_table, sin_table = rotary_tables(own_pos, ROT)
    queries = rotate(projected[:, :, 0] + bias_pair[:, 0], cos_table, sin_table, ROT).astype(
        jnp.bfloat16
    )
    keys_rot = rotate(projected[:, :, 1], cos_table, sin_table, ROT).astype(jnp.bfloat16)
    values_in = (projected[:, :, 2] + bias_pair[:, 1]).astype(jnp.bfloat16)
    kv_flat = jnp.concatenate(
        [keys_rot.reshape(tok_rows, head_cols), values_in.reshape(tok_rows, head_cols)], axis=-1
    )

    def split_keys(kv_piece):
        piece_rows = kv_piece.shape[0]
        group_rows = math.gcd(piece_rows, 4 * tok_rows)
        block_count = piece_rows // group_rows
        key_pos = positions.reshape(block_count, group_rows)
        key_blocks = kv_piece[:, :head_cols].reshape(block_count, group_rows, local_heads, HD)
        value_blocks = kv_piece[:, head_cols:].reshape(block_count, group_rows, local_heads, HD)
        return (key_blocks, value_blocks, key_pos)

    def key_block(state_in, block_in):
        key_blk, value_blk, key_pos = block_in
        run_max, run_total, run_acc = state_in
        scores = (
            jnp.einsum("qhd,khd->hqk", queries, key_blk, preferred_element_type=jnp.float32)
            * score_scale
        )
        allowed = (key_pos[None, :] <= own_pos[:, None])[None]
        scores = jnp.where(allowed, scores, NEG)
        new_max = jnp.maximum(run_max, jnp.max(scores, axis=-1))
        weights = jnp.where(allowed, jnp.exp(scores - new_max[..., None]), 0.0)
        factor = jnp.exp(run_max - new_max)
        run_total = run_total * factor + jnp.sum(weights, axis=-1)
        run_acc = run_acc * factor[..., None] + jnp.einsum(
            "hqk,khd->hqd",
            weights.astype(jnp.bfloat16),
            value_blk,
            preferred_element_type=jnp.float32,
        )
        return ((new_max, run_total, run_acc), None)

    start_state = (
        jnp.full((local_heads, tok_rows), NEG, jnp.float32),
        jnp.zeros((local_heads, tok_rows), jnp.float32),
        jnp.zeros((local_heads, tok_rows, HD), jnp.float32),
    )
    state_out, unused = lax.scan(
        key_block, start_state, split_keys(lax.all_gather(kv_flat, "ctx", axis=0, tiled=True))
    )
    run_max, run_total, run_acc = state_out
    attn_out = (
        jnp.transpose(run_acc / run_total[..., None], (1, 0, 2))
        .reshape(tok_rows, head_cols)
        .astype(jnp.bfloat16)
    )
    log_total = run_max + jnp.log(run_total)
    attn_part = jnp.einsum("tc,dc->td", attn_out, full_dense, preferred_element_type=jnp.float32)
    hidden_pre = jnp.dot(mlp_in, full_up, preferred_element_type=jnp.float32) + up_bias
    activated = gelu_value(hidden_pre).astype(jnp.bfloat16)
    mlp_part = jnp.einsum("tf,df->td", activated, full_down, preferred_element_type=jnp.float32)
    branches = lax.psum(attn_part + mlp_part, "tp")
    layer_out = (inputs + out_bias + branches).astype(jnp.bfloat16)
    cotangent = grad_out[0]
    cot_float = cotangent.astype(jnp.float32)
    out_bias_grad = jnp.sum(cot_float, axis=0)
    down_grad = jnp.einsum("td,tf->df", cotangent, activated, preferred_element_type=jnp.float32)
    pre_grad = jnp.dot(cotangent, full_down, preferred_element_type=jnp.float32) * gelu_slope(
        hidden_pre
    )
    up_bias_grad = jnp.sum(pre_grad, axis=0)
    pre_grad_b = pre_grad.astype(jnp.bfloat16)
    up_grad = jnp.einsum("td,tf->df", mlp_in, pre_grad_b, preferred_element_type=jnp.float32)
    normed_two_grad = jnp.einsum(
        "tf,df->td", pre_grad_b, full_up, preferred_element_type=jnp.float32
    )
    dense_grad = jnp.einsum("td,tc->dc", cotangent, attn_out, preferred_element_type=jnp.float32)
    out_grad = (
        jnp.dot(cotangent, full_dense, preferred_element_type=jnp.float32)
        .astype(jnp.bfloat16)
        .reshape(tok_rows, local_heads, HD)
    )
    row_delta = jnp.sum(
        out_grad.astype(jnp.float32)
        * attn_out.reshape(tok_rows, local_heads, HD).astype(jnp.float32),
        axis=-1,
    ).T
    back_kv = lax.all_gather(kv_flat, "ctx", axis=0, tiled=True)

    def pair_grads(key_blk, value_blk, key_pos):
        scores = (
            jnp.einsum("qhd,khd->hqk", queries, key_blk, preferred_element_type=jnp.float32)
            * score_scale
        )
        allowed = (key_pos[None, :] <= own_pos[:, None])[None]
        prob_table = jnp.where(
            allowed, jnp.exp(jnp.where(allowed, scores, NEG) - log_total[..., None]), 0.0
        )
        prob_grad = jnp.einsum(
            "qhd,khd->hqk", out_grad, value_blk, preferred_element_type=jnp.float32
        )
        score_grad = (prob_table * (prob_grad - row_delta[..., None])).astype(jnp.bfloat16)
        return (prob_table, score_grad)

    def grad_block(query_acc, block_in):
        key_blk, value_blk, key_pos = block_in
        prob_table, score_grad = pair_grads(key_blk, value_blk, key_pos)
        query_acc = (
            query_acc
            + jnp.einsum("hqk,khd->hqd", score_grad, key_blk, preferred_element_type=jnp.float32)
            * score_scale
        )
        key_part = (
            jnp.einsum("hqk,qhd->khd", score_grad, queries, preferred_element_type=jnp.float32)
            * score_scale
        )
        value_part = jnp.einsum(
            "hqk,qhd->khd",
            prob_table.astype(jnp.bfloat16),
            out_grad,
            preferred_element_type=jnp.float32,
        )
        group_rows = key_blk.shape[0]
        return (
            query_acc,
            jnp.concatenate(
                [
                    key_part.reshape(group_rows, head_cols),
                    value_part.reshape(group_rows, head_cols),
                ],
                axis=-1,
            ),
        )

    query_acc, kv_terms = lax.scan(
        grad_block, jnp.zeros((local_heads, tok_rows, HD), jnp.float32), split_keys(back_kv)
    )
    kv_grads = lax.psum_scatter(
        kv_terms.reshape(back_kv.shape[0], 2 * head_cols), "ctx", scatter_dimension=0, tiled=True
    )
    key_grad = kv_grads[:, :head_cols].reshape(tok_rows, local_heads, HD)
    value_grad = kv_grads[:, head_cols:].reshape(tok_rows, local_heads, HD)
    query_pre = rotate(jnp.transpose(query_acc, (1, 0, 2)), cos_table, -sin_table, ROT)
    key_pre = rotate(key_grad, cos_table, -sin_table, ROT)
    qv_grad = jnp.stack([jnp.sum(query_pre, axis=0), jnp.sum(value_grad, axis=0)], axis=1).reshape(
        -1
    )
    proj_grad = (
        jnp.stack([query_pre, key_pre, value_grad], axis=2)
        .reshape(tok_rows, 3 * head_cols)
        .astype(jnp.bfloat16)
    )
    qkv_grad = jnp.einsum("td,tc->dc", attn_in, proj_grad, preferred_element_type=jnp.float32)
    normed_one_grad = jnp.einsum(
        "tc,dc->td", proj_grad, full_qkv, preferred_element_type=jnp.float32
    )
    full_one, full_two = lax.psum((normed_one_grad, normed_two_grad), "tp")
    gain_part = jnp.stack(
        [jnp.sum(full_one * hat_one, axis=0), jnp.sum(full_two * hat_two, axis=0)]
    )
    bias_part = jnp.stack([jnp.sum(full_one, axis=0), jnp.sum(full_two, axis=0)])
    input_grad = (
        cot_float
        + norm_back(full_one, hat_one, inv_one, norm_gains[0])
        + norm_back(full_two, hat_two, inv_two, norm_gains[1])
    ).astype(jnp.bfloat16)
    gains_total, biases_total, qv_total, up_bias_total, out_bias_total = lax.psum(
        (gain_part, bias_part, qv_grad, up_bias_grad, out_bias_grad), ("dp", "ctx")
    )
    qkv_total, dense_total, up_total, down_total = (
        lax.psum_scatter(qkv_grad, ("dp", "ctx"), scatter_dimension=0, tiled=True),
        lax.psum_scatter(dense_grad, ("dp", "ctx"), scatter_dimension=0, tiled=True),
        lax.psum_scatter(up_grad, ("dp", "ctx"), scatter_dimension=0, tiled=True),
        lax.psum_scatter(down_grad, ("dp", "ctx"), scatter_dimension=0, tiled=True),
    )
    return (
        layer_out[None],
        input_grad[None],
        gains_total,
        biases_total,
        qkv_total,
        qv_total,
        dense_total,
        up_total,
        up_bias_total,
        down_total,
        out_bias_total,
    )


BF = jnp.bfloat16
F32 = jnp.float32


def mm(a, b, ca=1, cb=0):
    return lax.dot_general(a, b, (((ca,), (cb,)), ((), ())), preferred_element_type=F32)


def turn(x, cos_w, sin_a, sin_b):
    width = x.shape[1]
    return x * cos_w + pltpu.roll(x, width - ROT // 2, 1) * sin_a + pltpu.roll(x, ROT // 2, 1) * sin_b


def block_kernel(
    tp,
    heads,
    n_copies,
    x_ref,
    span_ref,
    gain_ref,
    shift_ref,
    wqkv_ref,
    qvb_ref,
    wdense_ref,
    wup_ref,
    upb_ref,
    wdown_ref,
    outb_ref,
    g_ref,
    cos_ref,
    sina_ref,
    sinb_ref,
    layer_out,
    grad_in,
    small_out,
    qkv_out,
    dense_out,
    up_out,
    down_out,
    qkv_w,
    dense_w,
    up_w,
    down_w,
    kv_f,
    xhat_s,
    inv_s,
    z1t_s,
    z2t_s,
    gt_s,
    attn_t,
    dq_t,
    dkv_g,
    dkv_bufs,
    qkv_g,
    qkv_bufs,
    dense_g,
    dense_bufs,
    up_g,
    up_bufs,
    down_g,
    down_bufs,
    out_g,
    out_snd,
    out_rcv,
    out_fin,
    t_g,
    t_snd,
    t_rcv,
    t_fin,
    sm_z,
    sm_p,
    ssem,
    rsem,
):
    c, t, z = lax.axis_index("dp"), lax.axis_index("ctx"), lax.axis_index("tp")
    xi, yi = t % 2, t // 2
    tx, ty, td = t + 1 - 2 * xi, t + 2 - 4 * yi, 3 - t
    to_x, to_y, to_d, to_c = (c, tx, z), (c, ty, z), (c, td, z), (1 - c, t, z)
    tok = x_ref.shape[0] * x_ref.shape[1]
    feat = x_ref.shape[2]
    spans = tok // SPAN
    hc = heads * HD

    barrier = pltpu.get_barrier_semaphore()
    peers = [to_c, to_x, to_y, to_d] + [(1 - c, o, z) for o in (tx, ty, td)]
    z_peers = [(c, t, (z + d) % tp) for d in range(1, tp)]
    for dev in peers + z_peers:
        pl.semaphore_signal(barrier, inc=1, device_id=dev, device_id_type=pl.DeviceIdType.MESH)
    pl.semaphore_wait(barrier, len(peers + z_peers))

    copies = []

    def rcopy(src, dst, dev):
        i = len(copies)
        cp = pltpu.make_async_remote_copy(
            src_ref=src,
            dst_ref=dst,
            send_sem=ssem.at[i],
            recv_sem=rsem.at[i],
            device_id=dev,
            device_id_type=pl.DeviceIdType.MESH,
        )
        cp.start()
        copies.append(cp)
        return cp

    class Gather:
        def __init__(self, own, full, cores=True):
            self.full, self.cores = full, cores
            self.base = 4 * c if cores else 0
            me = self.base + t
            if own is None:
                own = full.at[me]
            else:
                full[me] = own[...]
            self.half = full.shape[1] // 2
            self.cx = rcopy(own, full.at[me], to_x)
            self.cy = rcopy(own, full.at[me], to_y)
            self.cc = [rcopy(own, full.at[me], to_c)] if cores else []

        def relay(self):
            full, h = self.full, self.half
            sx, sy = self.base + tx, self.base + ty
            self.cx.wait_recv()
            a = full.at[sx, pl.ds(0, h)]
            self.d1 = rcopy(a, a, to_y)
            if self.cores:
                self.cc.append(rcopy(full.at[sx], full.at[sx], to_c))
            self.cy.wait_recv()
            b = full.at[sy, pl.ds(h, h)]
            self.d2 = rcopy(b, b, to_x)
            if self.cores:
                self.cc.append(rcopy(full.at[sy], full.at[sy], to_c))

        def finish(self):
            sd = self.base + td
            self.d1.wait_recv()
            self.d2.wait_recv()
            if self.cores:
                self.cc.append(rcopy(self.full.at[sd], self.full.at[sd], to_c))
                for cp in self.cc:
                    cp.wait_recv()

        def value(self):
            s = self.full.shape
            return self.full[...].reshape(s[0] * s[1], s[2])

    class Scatter:
        def __init__(self, total, bufs, cores=True):
            self.g, self.b, self.cores = total, bufs, cores
            self.h = total.shape[1] // 2
            if cores:
                snd, rcv = bufs[:2]
                snd[...] = total[pl.ds(4 * (1 - c), 4)].astype(BF)
                self.cc = rcopy(snd, rcv, to_c)

        def first(self):
            a1, b1, ra1, rb1 = self.b[2:6]
            h = self.h
            if self.cores:
                self.cc.wait_recv()
                self.s = self.g.at[pl.ds(4 * c, 4)]
                self.s[...] = self.s[...] + self.b[1][...].astype(F32)
            else:
                self.s = self.g
            for k in range(2):
                a1[k] = self.s[2 * k + 1 - xi, pl.ds(0, h)].astype(BF)
                b1[k] = self.s[2 * (1 - yi) + k, pl.ds(h, h)].astype(BF)
            self.ca = rcopy(a1, ra1, to_x)
            self.cb = rcopy(b1, rb1, to_y)

        def second(self):
            ra1, rb1, a2, b2, ra2, rb2 = self.b[4:10]
            h = self.h
            self.ca.wait_recv()
            a2[...] = (self.s[2 * (1 - yi) + xi, pl.ds(0, h)] + ra1[1 - yi].astype(F32)).astype(BF)
            self.ca2 = rcopy(a2, ra2, to_y)
            self.cb.wait_recv()
            b2[...] = (self.s[2 * yi + 1 - xi, pl.ds(h, h)] + rb1[1 - xi].astype(F32)).astype(BF)
            self.cb2 = rcopy(b2, rb2, to_x)

        def finish(self):
            ra1, rb1, a2, b2, ra2, rb2 = self.b[4:10]
            h = self.h
            self.ca2.wait_recv()
            top = self.s[t, pl.ds(0, h)] + ra1[yi].astype(F32) + ra2[...].astype(F32)
            self.cb2.wait_recv()
            low = self.s[t, pl.ds(h, h)] + rb1[xi].astype(F32) + rb2[...].astype(F32)
            return top, low

    def z_scatter(total, snd, rcv):
        snd[...] = total[...].astype(BF)
        return [rcopy(snd.at[(z + d) % tp], rcv.at[d - 1], (c, t, (z + d) % tp)) for d in range(1, tp)]

    def z_sum(cps, total, rcv):
        acc = total[z]
        for d in range(1, tp):
            cps[d - 1].wait_recv()
            acc = acc + rcv[d - 1].astype(F32)
        return acc

    def z_gather(fin):
        return [rcopy(fin.at[z], fin.at[z], dev) for dev in z_peers]

    ag_qkv = Gather(wqkv_ref, qkv_w)
    ag_dense = Gather(wdense_ref, dense_w)

    x = x_ref[...].reshape(tok, feat).astype(F32)
    cen = x - jnp.mean(x, axis=-1, keepdims=True)
    inv = lax.rsqrt(jnp.mean(cen * cen, axis=-1, keepdims=True) + EPS)
    xhat = cen * inv
    xhat_s[...] = xhat.reshape(xhat_s.shape)
    inv_s[...] = jnp.broadcast_to(inv, (tok, 128)).reshape(inv_s.shape)
    z1 = (xhat * gain_ref[0:1, :] + shift_ref[0:1, :]).astype(BF)
    z2 = (xhat * gain_ref[1:2, :] + shift_ref[1:2, :]).astype(BF)
    g = g_ref[...].reshape(tok, feat)
    sm_z[z] = jnp.zeros(sm_z.shape[1:], F32)
    sm_p[4 * c + t] = jnp.zeros(sm_p.shape[1:], F32)

    ag_qkv.relay()
    ag_dense.relay()
    ag_qkv.finish()
    proj = mm(z1, ag_qkv.value())
    wide = cos_ref.shape[1]
    proj = jnp.concatenate([proj, jnp.zeros((tok, wide - proj.shape[1]), F32)], axis=1)
    qkv = turn(proj + qvb_ref[...], cos_ref[...], sina_ref[...], sinb_ref[...])
    queries = [(qkv[:, 192 * h : 192 * h + HD].astype(BF) * BF(0.125)) for h in range(heads)]
    kv_f[t] = jnp.concatenate([qkv[:, 192 * h + HD : 192 * h + 192] for h in range(heads)], axis=1).astype(BF)
    ag_kv = Gather(None, kv_f, cores=False)
    ag_up = Gather(wup_ref, up_w)
    ag_down = Gather(wdown_ref, down_w)
    gt_s[...] = g.T
    z1t_s[...] = z1.T
    z2t_s[...] = z2.T
    ag_dense.finish()
    dattn = mm(g, ag_dense.value()).astype(BF)
    dattn_t = dattn.T
    ag_kv.relay()
    ag_kv.finish()

    lane = lax.broadcasted_iota(jnp.int32, (1, SPAN), 1)
    own_pos = jnp.concatenate([span_ref[0, t * spans + i] * SPAN + lane for i in range(spans)], axis=1)
    row = lax.broadcasted_iota(jnp.int32, (SPAN, 1), 0)
    keys = 4 * tok
    masks = jnp.concatenate(
        [row + span_ref[0, i] * SPAN <= own_pos for i in range(keys // SPAN)], axis=0
    )
    for h in range(heads):
        kvh = kv_f[:, :, 128 * h : 128 * h + 128].reshape(keys, 128)
        k, v = kvh[:, :HD], kvh[:, HD:]
        s = jnp.where(masks, mm(k, queries[h], 1, 1), NEG)
        e = jnp.exp(s - jnp.max(s, axis=0, keepdims=True))
        l_inv = 1.0 / jnp.sum(e, axis=0, keepdims=True)
        o_t = (mm(v, e.astype(BF), 0, 0) * l_inv).astype(BF)
        attn_t[h * HD : (h + 1) * HD, :] = o_t
        da_t = dattn_t[h * HD : (h + 1) * HD, :]
        delta = jnp.sum(da_t.astype(F32) * o_t.astype(F32), axis=0, keepdims=True)
        p = e * l_inv
        ds = (p * (mm(v, da_t) - delta)).astype(BF)
        dq_t[h * HD : (h + 1) * HD, :] = mm(k, ds, 0, 0) * 0.125
        dk = mm(ds, queries[h])
        dv = mm(p.astype(BF), dattn[:, h * HD : (h + 1) * HD])
        dkv_g[:, :, 128 * h : 128 * h + 128] = jnp.concatenate([dk, dv], axis=1).reshape(4, tok, 128)
        if h == 0:
            ag_up.relay()
        if h == 1:
            ag_down.relay()
    rs_kv = Scatter(dkv_g, dkv_bufs, cores=False)
    rs_kv.first()

    attn = attn_t[...].T
    dense_g[...] = mm(gt_s[...], attn).reshape(dense_g.shape)
    rs_dense = Scatter(dense_g, dense_bufs)
    ag_up.finish()
    pre = mm(z2, ag_up.value()) + upb_ref[...]
    phi = 0.5 * (1.0 + lax.erf(pre * (1.0 / math.sqrt(2.0))))
    act = (pre * phi).astype(BF)
    slope = phi + pre * jnp.exp(-0.5 * pre * pre) * (1.0 / math.sqrt(2.0 * math.pi))
    ag_down.finish()
    out_g[...] = (mm(attn, ag_dense.value(), 1, 1) + mm(act, ag_down.value(), 1, 1)).reshape(out_g.shape)
    z_out = z_scatter(out_g, out_snd, out_rcv)
    rs_kv.second()
    down_g[...] = mm(gt_s[...], act).reshape(down_g.shape)
    rs_down = Scatter(down_g, down_bufs)
    dpre = mm(g, ag_down.value()) * slope
    dpre_b = dpre.astype(BF)
    rs_dense.first()
    kv_top, kv_low = rs_kv.finish()
    dkv = jnp.concatenate([kv_top, kv_low], axis=0)
    dq = dq_t[...].T
    parts = []
    for h in range(heads):
        parts += [dq[:, h * HD : (h + 1) * HD], dkv[:, 128 * h : 128 * h + 128]]
    parts.append(jnp.zeros((tok, wide - 3 * hc), F32))
    dproj = turn(jnp.concatenate(parts, axis=1), cos_ref[...], -sina_ref[...], -sinb_ref[...])
    dproj_b = dproj.astype(BF)[:, : 3 * hc]
    dz1 = mm(dproj_b, ag_qkv.value(), 1, 1)
    dz2 = mm(dpre_b, ag_up.value(), 1, 1)
    t_g[...] = (dz1 * gain_ref[0:1, :] + dz2 * gain_ref[1:2, :]).reshape(t_g.shape)
    z_t = z_scatter(t_g, t_snd, t_rcv)
    xhat = xhat_s[...].reshape(tok, feat)
    sm_z[z, 0:1, :] = jnp.sum(dz1 * xhat, axis=0, keepdims=True)
    sm_z[z, 1:2, :] = jnp.sum(dz2 * xhat, axis=0, keepdims=True)
    sm_z[z, 2:3, :] = jnp.sum(dz1, axis=0, keepdims=True)
    sm_z[z, 3:4, :] = jnp.sum(dz2, axis=0, keepdims=True)
    c_sm = z_gather(sm_z)
    rs_down.first()
    up_g[...] = mm(z2t_s[...], dpre_b).reshape(up_g.shape)
    rs_up = Scatter(up_g, up_bufs)
    qkv_g[...] = mm(z1t_s[...], dproj_b).reshape(qkv_g.shape)
    rs_qkv = Scatter(qkv_g, qkv_bufs)
    rs_dense.second()
    fin = z_sum(z_out, out_g, out_rcv)
    out_fin[z] = (x_ref[z].astype(F32) + outb_ref[...] + fin).astype(BF)
    c_out = z_gather(out_fin)
    rs_up.first()
    rs_qkv.first()
    for cp in c_sm:
        cp.wait_recv()
    me = 4 * c + t
    sm = sm_z[0]
    for i in range(1, tp):
        sm = sm + sm_z[i]
    sm_p[me] = sm
    sm_p[me, 4:5, :] = jnp.sum(g.astype(F32), axis=0, keepdims=True)
    sm_p[me, 5:6, 0 : dpre.shape[1]] = jnp.sum(dpre, axis=0, keepdims=True)
    sm_p[me, 6:7, 0:wide] = jnp.sum(dproj, axis=0, keepdims=True)
    c_pl = [rcopy(sm_p.at[me], sm_p.at[me], dev) for dev in peers]
    rs_down.second()
    tt = z_sum(z_t, t_g, t_rcv)
    xh = xhat_s[z]
    back = inv_s[z, :, 0:1] * (
        tt - jnp.mean(tt, axis=-1, keepdims=True) - xh * jnp.mean(tt * xh, axis=-1, keepdims=True)
    )
    t_fin[z] = (g_ref[z].astype(F32) + back).astype(BF)
    c_t = z_gather(t_fin)
    rs_up.second()
    rs_qkv.second()
    for rs, out in ((rs_dense, dense_out), (rs_down, down_out), (rs_up, up_out), (rs_qkv, qkv_out)):
        top, low = rs.finish()
        out[pl.ds(0, rs.h), :] = top
        out[pl.ds(rs.h, rs.h), :] = low
    for cp in c_pl:
        cp.wait_recv()
    sm = sm_p[0]
    for i in range(1, 8):
        sm = sm + sm_p[i]
    small_out[...] = sm
    for cp in c_out:
        cp.wait_recv()
    layer_out[...] = out_fin[...]
    for cp in c_t:
        cp.wait_recv()
    grad_in[...] = t_fin[...]
    assert len(copies) <= n_copies
    for cp in copies:
        cp.wait_send()


def one_kernel(tp, *args):
    x, span, gains, shifts, wqkv, qvb, wdense, wup, upb, wdown, outb, g = args
    tok, feat = x.shape[1:]
    rows = wqkv.shape[0]
    heads = qvb.shape[0] // (2 * HD)
    ff = wup.shape[1]
    spans = tok // SPAN
    wide = -(-3 * heads * HD // 128) * 128
    own = lax.dynamic_slice_in_dim(span[0], lax.axis_index("ctx") * spans, spans)
    pos = (own[:, None] * SPAN + jnp.arange(SPAN, dtype=jnp.int32)[None, :]).reshape(-1)
    cos_t, sin_t = rotary_tables(pos, ROT)
    col = jnp.arange(wide) % (3 * HD)
    turned = (col < 2 * HD) & (jnp.arange(wide) < 3 * heads * HD)
    low = turned & (col % HD < ROT // 2)
    high = turned & (col % HD >= ROT // 2) & (col % HD < ROT)
    reps = wide // (ROT // 2)
    cos_w = jnp.where(low | high, jnp.tile(cos_t, (1, reps)), 1.0)
    sin_w = jnp.tile(sin_t, (1, reps))
    sin_a = jnp.where(low, -sin_w, 0.0)
    sin_b = jnp.where(high, sin_w, 0.0)
    pair = qvb.reshape(heads, 2, HD)
    bias = jnp.stack([pair[:, 0], jnp.zeros_like(pair[:, 0]), pair[:, 1]], axis=1).reshape(1, -1)
    bias = jnp.pad(bias, ((0, 0), (0, wide - bias.shape[1])))
    piece = tok // tp
    cols = (wqkv.shape[1], wdense.shape[1], ff, ff)
    kvw = 2 * heads * HD

    def bufs(r, w, cores=True):
        h = r // 2
        first = [pltpu.VMEM((4, r, w), BF)] * 2 if cores else [pltpu.VMEM((8, 128), F32)] * 2
        return tuple(first + [pltpu.VMEM((2, h, w), BF)] * 4 + [pltpu.VMEM((h, w), BF)] * 4)

    vm = pltpu.VMEM
    scratch = [vm((8, rows, w), BF) for w in cols]
    scratch += [
        vm((4, tok, kvw), BF),
        vm((tp, piece, feat), F32),
        vm((tp, piece, 128), F32),
        vm((feat, tok), BF),
        vm((feat, tok), BF),
        vm((feat, tok), BF),
        vm((heads * HD, tok), BF),
        vm((heads * HD, tok), F32),
        vm((4, tok, kvw), F32),
        bufs(tok, kvw, False),
    ]
    for w in cols:
        scratch += [vm((8, rows, w), F32), bufs(rows, w)]
    for i in range(2):
        scratch += [
            vm((tp, piece, feat), F32),
            vm((tp, piece, feat), BF),
            vm((tp - 1, piece, feat), BF),
            vm((tp, piece, feat), BF),
        ]
    n_copies = 128
    scratch += [
        vm((tp, 8, feat), F32),
        vm((8, 8, feat), F32),
        pltpu.SemaphoreType.DMA((n_copies,)),
        pltpu.SemaphoreType.DMA((n_copies,)),
    ]
    vspec = pl.BlockSpec(memory_space=pltpu.VMEM)
    specs = [vspec] * 15
    specs[1] = pl.BlockSpec(memory_space=pltpu.SMEM)
    sds = jax.ShapeDtypeStruct
    layer_out, grad_in, small, gqkv, gdense, gup, gdown = pl.pallas_call(
        functools.partial(block_kernel, tp, heads, n_copies),
        out_shape=(
            sds((tp, piece, feat), BF),
            sds((tp, piece, feat), BF),
            sds((8, feat), F32),
        )
        + tuple(sds((rows, w), F32) for w in cols),
        in_specs=specs,
        out_specs=tuple([vspec] * 7),
        scratch_shapes=scratch,
        compiler_params=pltpu.CompilerParams(
            collective_id=0, has_side_effects=True, vmem_limit_bytes=60 * 1024 * 1024
        ),
    )(
        x.reshape(tp, piece, feat),
        span,
        gains,
        shifts,
        wqkv,
        bias,
        wdense,
        wup,
        upb[None],
        wdown,
        outb[None],
        g.reshape(tp, piece, feat),
        cos_w,
        sin_a,
        sin_b,
    )
    qv = small[6, : 3 * heads * HD].reshape(heads, 3, HD)[:, 0::2].reshape(-1)
    return (
        layer_out.reshape(1, tok, feat),
        grad_in.reshape(1, tok, feat),
        small[0:2],
        small[2:4],
        gqkv,
        qv,
        gdense,
        gup,
        small[5, :ff],
        gdown,
        small[4],
    )


def solution(mesh):
    placed = (
        P("dp", "ctx", None),
        P("dp", None),
        P(),
        P(),
        P(("dp", "ctx"), "tp"),
        P("tp"),
        P(("dp", "ctx"), "tp"),
        P(("dp", "ctx"), "tp"),
        P("tp"),
        P(("dp", "ctx"), "tp"),
        P(),
        P("dp", "ctx", None),
    )
    sizes = dict(mesh.shape)
    body = on_device
    if sizes["dp"] == 2 and sizes["ctx"] == 4:
        body = functools.partial(one_kernel, sizes["tp"])
    return jax.shard_map(
        body,
        mesh=mesh,
        in_specs=placed,
        out_specs=(
            P("dp", "ctx", None),
            P("dp", "ctx", None),
            P(),
            P(),
            P(("dp", "ctx"), "tp"),
            P("tp"),
            P(("dp", "ctx"), "tp"),
            P(("dp", "ctx"), "tp"),
            P("tp"),
            P(("dp", "ctx"), "tp"),
            P(),
        ),
        check_vma=False,
    )
```

```python
import functools
import math

import jax
import jax.numpy as jnp
from jax import lax
from jax.experimental import pallas as pl
from jax.experimental.pallas import tpu as pltpu
from jax.sharding import PartitionSpec as P

HD = 64
ROT = 16
SPAN = 128


EPS = 1e-05
NEG = -1e30


def layer_norm(values, gain_vec, shift_vec):
    row_mean = jnp.mean(values, axis=-1, keepdims=True)
    centered = values - row_mean
    variance = jnp.mean(centered * centered, axis=-1, keepdims=True)
    inv_std = lax.rsqrt(variance + EPS)
    normed = centered * inv_std
    return (normed * gain_vec + shift_vec, normed, inv_std)


def norm_back(grad_normed, normed, inv_std, gain_vec):
    scaled = grad_normed * gain_vec
    return inv_std * (
        scaled
        - jnp.mean(scaled, axis=-1, keepdims=True)
        - normed * jnp.mean(scaled * normed, axis=-1, keepdims=True)
    )


def rotary_tables(positions, rot_dims):
    half_rot = rot_dims // 2
    frequency = 1.0 / 10000.0 ** (jnp.arange(half_rot, dtype=jnp.float32) * (2.0 / rot_dims))
    angles = positions.astype(jnp.float32)[:, None] * frequency[None, :]
    return (jnp.cos(angles), jnp.sin(angles))


def rotate(vectors, cos_table, sin_table, rot_dims):
    half_rot = rot_dims // 2
    front_half = vectors[..., :half_rot]
    back_half = vectors[..., half_rot:rot_dims]
    cos_row = cos_table[:, None, :]
    sin_row = sin_table[:, None, :]
    return jnp.concatenate(
        [
            front_half * cos_row - back_half * sin_row,
            back_half * cos_row + front_half * sin_row,
            vectors[..., rot_dims:],
        ],
        axis=-1,
    )


def gelu_value(hidden):
    return 0.5 * hidden * (1.0 + jax.scipy.special.erf(hidden * (1.0 / math.sqrt(2.0))))


def gelu_slope(hidden):
    return 0.5 * (1.0 + jax.scipy.special.erf(hidden * (1.0 / math.sqrt(2.0)))) + hidden * jnp.exp(
        -0.5 * hidden * hidden
    ) * (1.0 / math.sqrt(2.0 * math.pi))


def on_device(
    hidden_in,
    span_order,
    norm_gains,
    norm_biases,
    w_qkv,
    qv_bias,
    w_dense,
    w_up,
    up_bias,
    w_down,
    out_bias,
    grad_out,
):
    tok_rows = hidden_in.shape[1]
    local_heads = qv_bias.shape[0] // (2 * HD)
    head_cols = local_heads * HD
    score_scale = 1.0 / math.sqrt(HD)
    positions = (
        span_order[0][:, None] * SPAN + jnp.arange(SPAN, dtype=jnp.int32)[None, :]
    ).reshape(-1)
    own_pos = lax.dynamic_slice_in_dim(positions, lax.axis_index("ctx") * tok_rows, tok_rows)
    full_qkv, full_dense, full_up, full_down = (
        lax.all_gather(w_qkv, ("dp", "ctx"), axis=0, tiled=True),
        lax.all_gather(w_dense, ("dp", "ctx"), axis=0, tiled=True),
        lax.all_gather(w_up, ("dp", "ctx"), axis=0, tiled=True),
        lax.all_gather(w_down, ("dp", "ctx"), axis=0, tiled=True),
    )
    inputs = hidden_in[0].astype(jnp.float32)
    normed_one, hat_one, inv_one = layer_norm(inputs, norm_gains[0], norm_biases[0])
    normed_two, hat_two, inv_two = layer_norm(inputs, norm_gains[1], norm_biases[1])
    attn_in = normed_one.astype(jnp.bfloat16)
    mlp_in = normed_two.astype(jnp.bfloat16)
    projected = jnp.dot(attn_in, full_qkv, preferred_element_type=jnp.float32).reshape(
        tok_rows, local_heads, 3, HD
    )
    bias_pair = qv_bias.reshape(local_heads, 2, HD)
    cos_table, sin_table = rotary_tables(own_pos, ROT)
    queries = rotate(projected[:, :, 0] + bias_pair[:, 0], cos_table, sin_table, ROT).astype(
        jnp.bfloat16
    )
    keys_rot = rotate(projected[:, :, 1], cos_table, sin_table, ROT).astype(jnp.bfloat16)
    values_in = (projected[:, :, 2] + bias_pair[:, 1]).astype(jnp.bfloat16)
    kv_flat = jnp.concatenate(
        [keys_rot.reshape(tok_rows, head_cols), values_in.reshape(tok_rows, head_cols)], axis=-1
    )

    def split_keys(kv_piece):
        piece_rows = kv_piece.shape[0]
        group_rows = math.gcd(piece_rows, 4 * tok_rows)
        block_count = piece_rows // group_rows
        key_pos = positions.reshape(block_count, group_rows)
        key_blocks = kv_piece[:, :head_cols].reshape(block_count, group_rows, local_heads, HD)
        value_blocks = kv_piece[:, head_cols:].reshape(block_count, group_rows, local_heads, HD)
        return (key_blocks, value_blocks, key_pos)

    def key_block(state_in, block_in):
        key_blk, value_blk, key_pos = block_in
        run_max, run_total, run_acc = state_in
        scores = (
            jnp.einsum("qhd,khd->hqk", queries, key_blk, preferred_element_type=jnp.float32)
            * score_scale
        )
        allowed = (key_pos[None, :] <= own_pos[:, None])[None]
        scores = jnp.where(allowed, scores, NEG)
        new_max = jnp.maximum(run_max, jnp.max(scores, axis=-1))
        weights = jnp.where(allowed, jnp.exp(scores - new_max[..., None]), 0.0)
        factor = jnp.exp(run_max - new_max)
        run_total = run_total * factor + jnp.sum(weights, axis=-1)
        run_acc = run_acc * factor[..., None] + jnp.einsum(
            "hqk,khd->hqd",
            weights.astype(jnp.bfloat16),
            value_blk,
            preferred_element_type=jnp.float32,
        )
        return ((new_max, run_total, run_acc), None)

    start_state = (
        jnp.full((local_heads, tok_rows), NEG, jnp.float32),
        jnp.zeros((local_heads, tok_rows), jnp.float32),
        jnp.zeros((local_heads, tok_rows, HD), jnp.float32),
    )
    state_out, unused = lax.scan(
        key_block, start_state, split_keys(lax.all_gather(kv_flat, "ctx", axis=0, tiled=True))
    )
    run_max, run_total, run_acc = state_out
    attn_out = (
        jnp.transpose(run_acc / run_total[..., None], (1, 0, 2))
        .reshape(tok_rows, head_cols)
        .astype(jnp.bfloat16)
    )
    log_total = run_max + jnp.log(run_total)
    attn_part = jnp.einsum("tc,dc->td", attn_out, full_dense, preferred_element_type=jnp.float32)
    hidden_pre = jnp.dot(mlp_in, full_up, preferred_element_type=jnp.float32) + up_bias
    activated = gelu_value(hidden_pre).astype(jnp.bfloat16)
    mlp_part = jnp.einsum("tf,df->td", activated, full_down, preferred_element_type=jnp.float32)
    branches = lax.psum(attn_part + mlp_part, "tp")
    layer_out = (inputs + out_bias + branches).astype(jnp.bfloat16)
    cotangent = grad_out[0]
    cot_float = cotangent.astype(jnp.float32)
    out_bias_grad = jnp.sum(cot_float, axis=0)
    down_grad = jnp.einsum("td,tf->df", cotangent, activated, preferred_element_type=jnp.float32)
    pre_grad = jnp.dot(cotangent, full_down, preferred_element_type=jnp.float32) * gelu_slope(
        hidden_pre
    )
    up_bias_grad = jnp.sum(pre_grad, axis=0)
    pre_grad_b = pre_grad.astype(jnp.bfloat16)
    up_grad = jnp.einsum("td,tf->df", mlp_in, pre_grad_b, preferred_element_type=jnp.float32)
    normed_two_grad = jnp.einsum(
        "tf,df->td", pre_grad_b, full_up, preferred_element_type=jnp.float32
    )
    dense_grad = jnp.einsum("td,tc->dc", cotangent, attn_out, preferred_element_type=jnp.float32)
    out_grad = (
        jnp.dot(cotangent, full_dense, preferred_element_type=jnp.float32)
        .astype(jnp.bfloat16)
        .reshape(tok_rows, local_heads, HD)
    )
    row_delta = jnp.sum(
        out_grad.astype(jnp.float32)
        * attn_out.reshape(tok_rows, local_heads, HD).astype(jnp.float32),
        axis=-1,
    ).T
    back_kv = lax.all_gather(kv_flat, "ctx", axis=0, tiled=True)

    def pair_grads(key_blk, value_blk, key_pos):
        scores = (
            jnp.einsum("qhd,khd->hqk", queries, key_blk, preferred_element_type=jnp.float32)
            * score_scale
        )
        allowed = (key_pos[None, :] <= own_pos[:, None])[None]
        prob_table = jnp.where(
            allowed, jnp.exp(jnp.where(allowed, scores, NEG) - log_total[..., None]), 0.0
        )
        prob_grad = jnp.einsum(
            "qhd,khd->hqk", out_grad, value_blk, preferred_element_type=jnp.float32
        )
        score_grad = (prob_table * (prob_grad - row_delta[..., None])).astype(jnp.bfloat16)
        return (prob_table, score_grad)

    def grad_block(query_acc, block_in):
        key_blk, value_blk, key_pos = block_in
        prob_table, score_grad = pair_grads(key_blk, value_blk, key_pos)
        query_acc = (
            query_acc
            + jnp.einsum("hqk,khd->hqd", score_grad, key_blk, preferred_element_type=jnp.float32)
            * score_scale
        )
        key_part = (
            jnp.einsum("hqk,qhd->khd", score_grad, queries, preferred_element_type=jnp.float32)
            * score_scale
        )
        value_part = jnp.einsum(
            "hqk,qhd->khd",
            prob_table.astype(jnp.bfloat16),
            out_grad,
            preferred_element_type=jnp.float32,
        )
        group_rows = key_blk.shape[0]
        return (
            query_acc,
            jnp.concatenate(
                [
                    key_part.reshape(group_rows, head_cols),
                    value_part.reshape(group_rows, head_cols),
                ],
                axis=-1,
            ),
        )

    query_acc, kv_terms = lax.scan(
        grad_block, jnp.zeros((local_heads, tok_rows, HD), jnp.float32), split_keys(back_kv)
    )
    kv_grads = lax.psum_scatter(
        kv_terms.reshape(back_kv.shape[0], 2 * head_cols), "ctx", scatter_dimension=0, tiled=True
    )
    key_grad = kv_grads[:, :head_cols].reshape(tok_rows, local_heads, HD)
    value_grad = kv_grads[:, head_cols:].reshape(tok_rows, local_heads, HD)
    query_pre = rotate(jnp.transpose(query_acc, (1, 0, 2)), cos_table, -sin_table, ROT)
    key_pre = rotate(key_grad, cos_table, -sin_table, ROT)
    qv_grad = jnp.stack([jnp.sum(query_pre, axis=0), jnp.sum(value_grad, axis=0)], axis=1).reshape(
        -1
    )
    proj_grad = (
        jnp.stack([query_pre, key_pre, value_grad], axis=2)
        .reshape(tok_rows, 3 * head_cols)
        .astype(jnp.bfloat16)
    )
    qkv_grad = jnp.einsum("td,tc->dc", attn_in, proj_grad, preferred_element_type=jnp.float32)
    normed_one_grad = jnp.einsum(
        "tc,dc->td", proj_grad, full_qkv, preferred_element_type=jnp.float32
    )
    full_one, full_two = lax.psum((normed_one_grad, normed_two_grad), "tp")
    gain_part = jnp.stack(
        [jnp.sum(full_one * hat_one, axis=0), jnp.sum(full_two * hat_two, axis=0)]
    )
    bias_part = jnp.stack([jnp.sum(full_one, axis=0), jnp.sum(full_two, axis=0)])
    input_grad = (
        cot_float
        + norm_back(full_one, hat_one, inv_one, norm_gains[0])
        + norm_back(full_two, hat_two, inv_two, norm_gains[1])
    ).astype(jnp.bfloat16)
    gains_total, biases_total, qv_total, up_bias_total, out_bias_total = lax.psum(
        (gain_part, bias_part, qv_grad, up_bias_grad, out_bias_grad), ("dp", "ctx")
    )
    qkv_total, dense_total, up_total, down_total = (
        lax.psum_scatter(qkv_grad, ("dp", "ctx"), scatter_dimension=0, tiled=True),
        lax.psum_scatter(dense_grad, ("dp", "ctx"), scatter_dimension=0, tiled=True),
        lax.psum_scatter(up_grad, ("dp", "ctx"), scatter_dimension=0, tiled=True),
        lax.psum_scatter(down_grad, ("dp", "ctx"), scatter_dimension=0, tiled=True),
    )
    return (
        layer_out[None],
        input_grad[None],
        gains_total,
        biases_total,
        qkv_total,
        qv_total,
        dense_total,
        up_total,
        up_bias_total,
        down_total,
        out_bias_total,
    )


BF = jnp.bfloat16
F32 = jnp.float32


def mm(a, b, ca=1, cb=0):
    return lax.dot_general(a, b, (((ca,), (cb,)), ((), ())), preferred_element_type=F32)


def turn(x, cos_w, sin_a, sin_b):
    width = x.shape[1]
    return x * cos_w + pltpu.roll(x, width - ROT // 2, 1) * sin_a + pltpu.roll(x, ROT // 2, 1) * sin_b


def block_kernel(
    tp,
    heads,
    n_copies,
    x_ref,
    span_ref,
    gain_ref,
    shift_ref,
    wqkv_ref,
    qvb_ref,
    wdense_ref,
    wup_ref,
    upb_ref,
    wdown_ref,
    outb_ref,
    g_ref,
    layer_out,
    grad_in,
    small_out,
    qkv_out,
    dense_out,
    up_out,
    down_out,
    qkv_w,
    dense_w,
    up_w,
    down_w,
    kv_f,
    xhat_s,
    inv_s,
    z1t_s,
    z2t_s,
    gt_s,
    attn_t,
    dq_t,
    dkv_g,
    dkv_bufs,
    qkv_g,
    qkv_bufs,
    dense_g,
    dense_bufs,
    up_g,
    up_bufs,
    down_g,
    down_bufs,
    out_g,
    out_snd,
    out_rcv,
    out_fin,
    t_g,
    t_snd,
    t_rcv,
    t_fin,
    sm_z,
    sm_p,
    cos_ref,
    sina_ref,
    sinb_ref,
    ssem,
    rsem,
):
    c, t, z = lax.axis_index("dp"), lax.axis_index("ctx"), lax.axis_index("tp")
    xi, yi = t % 2, t // 2
    tx, ty, td = t + 1 - 2 * xi, t + 2 - 4 * yi, 3 - t
    to_x, to_y, to_d, to_c = (c, tx, z), (c, ty, z), (c, td, z), (1 - c, t, z)
    tok = x_ref.shape[0] * x_ref.shape[1]
    feat = x_ref.shape[2]
    spans = tok // SPAN
    hc = heads * HD

    barrier = pltpu.get_barrier_semaphore()
    peers = [to_c, to_x, to_y, to_d] + [(1 - c, o, z) for o in (tx, ty, td)]
    z_peers = [(c, t, (z + d) % tp) for d in range(1, tp)]
    for dev in peers + z_peers:
        pl.semaphore_signal(barrier, inc=1, device_id=dev, device_id_type=pl.DeviceIdType.MESH)
    pl.semaphore_wait(barrier, len(peers + z_peers))

    copies = []

    def rcopy(src, dst, dev):
        i = len(copies)
        cp = pltpu.make_async_remote_copy(
            src_ref=src,
            dst_ref=dst,
            send_sem=ssem.at[i],
            recv_sem=rsem.at[i],
            device_id=dev,
            device_id_type=pl.DeviceIdType.MESH,
        )
        cp.start()
        copies.append(cp)
        return cp

    class Gather:
        def __init__(self, own, full, cores=True):
            self.full, self.cores = full, cores
            self.base = 4 * c if cores else 0
            me = self.base + t
            if own is None:
                own = full.at[me]
            else:
                full[me] = own[...]
            self.half = full.shape[1] // 2
            self.cx = rcopy(own, full.at[me], to_x)
            self.cy = rcopy(own, full.at[me], to_y)
            self.cc = [rcopy(own, full.at[me], to_c)] if cores else []

        def relay(self):
            full, h = self.full, self.half
            sx, sy = self.base + tx, self.base + ty
            self.cx.wait_recv()
            a = full.at[sx, pl.ds(0, h)]
            self.d1 = rcopy(a, a, to_y)
            if self.cores:
                self.cc.append(rcopy(full.at[sx], full.at[sx], to_c))
            self.cy.wait_recv()
            b = full.at[sy, pl.ds(h, h)]
            self.d2 = rcopy(b, b, to_x)
            if self.cores:
                self.cc.append(rcopy(full.at[sy], full.at[sy], to_c))

        def finish(self):
            sd = self.base + td
            self.d1.wait_recv()
            self.d2.wait_recv()
            if self.cores:
                self.cc.append(rcopy(self.full.at[sd], self.full.at[sd], to_c))
                for cp in self.cc:
                    cp.wait_recv()

        def value(self):
            s = self.full.shape
            return self.full[...].reshape(s[0] * s[1], s[2])

    class Scatter:
        def __init__(self, total, bufs, cores=True):
            self.g, self.b, self.cores = total, bufs, cores
            self.h = total.shape[1] // 2
            if cores:
                snd, rcv = bufs[:2]
                snd[...] = total[pl.ds(4 * (1 - c), 4)].astype(BF)
                self.cc = rcopy(snd, rcv, to_c)

        def first(self):
            a1, b1, ra1, rb1 = self.b[2:6]
            h = self.h
            if self.cores:
                self.cc.wait_recv()
                self.s = self.g.at[pl.ds(4 * c, 4)]
                self.s[...] = self.s[...] + self.b[1][...].astype(F32)
            else:
                self.s = self.g
            for k in range(2):
                a1[k] = self.s[2 * k + 1 - xi, pl.ds(0, h)].astype(BF)
                b1[k] = self.s[2 * (1 - yi) + k, pl.ds(h, h)].astype(BF)
            self.ca = rcopy(a1, ra1, to_x)
            self.cb = rcopy(b1, rb1, to_y)

        def second(self):
            ra1, rb1, a2, b2, ra2, rb2 = self.b[4:10]
            h = self.h
            self.ca.wait_recv()
            a2[...] = (self.s[2 * (1 - yi) + xi, pl.ds(0, h)] + ra1[1 - yi].astype(F32)).astype(BF)
            self.ca2 = rcopy(a2, ra2, to_y)
            self.cb.wait_recv()
            b2[...] = (self.s[2 * yi + 1 - xi, pl.ds(h, h)] + rb1[1 - xi].astype(F32)).astype(BF)
            self.cb2 = rcopy(b2, rb2, to_x)

        def finish(self):
            ra1, rb1, a2, b2, ra2, rb2 = self.b[4:10]
            h = self.h
            self.ca2.wait_recv()
            top = self.s[t, pl.ds(0, h)] + ra1[yi].astype(F32) + ra2[...].astype(F32)
            self.cb2.wait_recv()
            low = self.s[t, pl.ds(h, h)] + rb1[xi].astype(F32) + rb2[...].astype(F32)
            return top, low

    def z_scatter(total, snd, rcv):
        snd[...] = total[...].astype(BF)
        return [rcopy(snd.at[(z + d) % tp], rcv.at[d - 1], (c, t, (z + d) % tp)) for d in range(1, tp)]

    def z_sum(cps, total, rcv):
        acc = total[z]
        for d in range(1, tp):
            cps[d - 1].wait_recv()
            acc = acc + rcv[d - 1].astype(F32)
        return acc

    def z_gather(fin):
        return [rcopy(fin.at[z], fin.at[z], dev) for dev in z_peers]

    ag_qkv = Gather(wqkv_ref, qkv_w)
    ag_dense = Gather(wdense_ref, dense_w)

    x = x_ref[...].reshape(tok, feat).astype(F32)
    cen = x - jnp.mean(x, axis=-1, keepdims=True)
    inv = lax.rsqrt(jnp.mean(cen * cen, axis=-1, keepdims=True) + EPS)
    xhat = cen * inv
    xhat_s[...] = xhat.reshape(xhat_s.shape)
    inv_s[...] = jnp.broadcast_to(inv, (tok, 128)).reshape(inv_s.shape)
    z1 = (xhat * gain_ref[0:1, :] + shift_ref[0:1, :]).astype(BF)
    z2 = (xhat * gain_ref[1:2, :] + shift_ref[1:2, :]).astype(BF)
    g = g_ref[...].reshape(tok, feat)
    lane = lax.broadcasted_iota(jnp.int32, (1, SPAN), 1)
    row = lax.broadcasted_iota(jnp.int32, (SPAN, 1), 0)
    wide = -(-3 * hc // 128) * 128
    col_pos = jnp.concatenate([span_ref[0, t * spans + i] * SPAN + row for i in range(spans)], axis=0)
    freq = jnp.zeros((1, 128), F32)
    for f in range(ROT // 2):
        step = 1.0 / 10000.0 ** (f * 2.0 / ROT)
        freq = jnp.where(lane % (ROT // 2) == f, step, freq)
    angle = col_pos.astype(F32) * freq
    reps = wide // 128
    cos_w = jnp.concatenate([jnp.cos(angle)] * reps, axis=1)
    sin_w = jnp.concatenate([jnp.sin(angle)] * reps, axis=1)
    col = lax.broadcasted_iota(jnp.int32, (1, wide), 1)
    turned = (col % (3 * HD) < 2 * HD) & (col < 3 * hc)
    lo = turned & (col % HD < ROT // 2)
    hi = turned & (col % HD >= ROT // 2) & (col % HD < ROT)
    cos_ref[...] = jnp.where(lo | hi, cos_w, 1.0)
    sina_ref[...] = jnp.where(lo, -sin_w, 0.0)
    sinb_ref[...] = jnp.where(hi, sin_w, 0.0)
    qvb = qvb_ref[...].reshape(1, 2 * hc)
    bias = []
    for h in range(heads):
        bias += [qvb[:, 128 * h : 128 * h + HD], jnp.zeros((1, HD), F32), qvb[:, 128 * h + HD : 128 * h + 128]]
    bias = jnp.concatenate(bias + [jnp.zeros((1, wide - 3 * hc), F32)], axis=1)
    sm_z[z] = jnp.zeros(sm_z.shape[1:], F32)
    sm_p[4 * c + t] = jnp.zeros(sm_p.shape[1:], F32)

    ag_qkv.relay()
    ag_up = Gather(wup_ref, up_w)
    ag_dense.relay()
    ag_qkv.finish()
    proj = mm(z1, ag_qkv.value())
    proj = jnp.concatenate([proj, jnp.zeros((tok, wide - proj.shape[1]), F32)], axis=1)
    qkv = turn(proj + bias, cos_ref[...], sina_ref[...], sinb_ref[...])
    queries = [(qkv[:, 192 * h : 192 * h + HD].astype(BF) * BF(0.125)) for h in range(heads)]
    kv_f[t] = jnp.concatenate([qkv[:, 192 * h + HD : 192 * h + 192] for h in range(heads)], axis=1).astype(BF)
    ag_kv = Gather(None, kv_f, cores=False)
    ag_dense.finish()
    dattn = mm(g, ag_dense.value()).astype(BF)
    dattn_t = dattn.T
    gt_s[...] = g.T
    ag_kv.relay()
    ag_up.relay()
    ag_down = Gather(wdown_ref, down_w)
    z1t_s[...] = z1.T
    z2t_s[...] = z2.T
    ag_up.finish()
    pre = mm(z2, ag_up.value()) + upb_ref[...].reshape(1, -1)
    phi = 0.5 * (1.0 + lax.erf(pre * (1.0 / math.sqrt(2.0))))
    act = (pre * phi).astype(BF)
    slope = phi + pre * jnp.exp(-0.5 * pre * pre) * (1.0 / math.sqrt(2.0 * math.pi))
    ag_kv.finish()

    own_pos = jnp.concatenate([span_ref[0, t * spans + i] * SPAN + lane for i in range(spans)], axis=1)
    keys = 4 * tok
    masks = jnp.concatenate(
        [row + span_ref[0, i] * SPAN <= own_pos for i in range(keys // SPAN)], axis=0
    )
    for h in range(heads):
        kvh = kv_f[:, :, 128 * h : 128 * h + 128].reshape(keys, 128)
        k, v = kvh[:, :HD], kvh[:, HD:]
        s = jnp.where(masks, mm(k, queries[h], 1, 1), NEG)
        e = jnp.exp(s - jnp.max(s, axis=0, keepdims=True))
        l_inv = 1.0 / jnp.sum(e, axis=0, keepdims=True)
        o_t = (mm(v, e.astype(BF), 0, 0) * l_inv).astype(BF)
        attn_t[h * HD : (h + 1) * HD, :] = o_t
        da_t = dattn_t[h * HD : (h + 1) * HD, :]
        delta = jnp.sum(da_t.astype(F32) * o_t.astype(F32), axis=0, keepdims=True)
        p = e * l_inv
        ds = (p * (mm(v, da_t) - delta)).astype(BF)
        dq_t[h * HD : (h + 1) * HD, :] = mm(k, ds, 0, 0) * 0.125
        dk = mm(ds, queries[h])
        dv = mm(p.astype(BF), dattn[:, h * HD : (h + 1) * HD])
        dkv_g[:, :, 128 * h : 128 * h + 128] = jnp.concatenate([dk, dv], axis=1).reshape(4, tok, 128)
        if h == 0:
            ag_down.relay()
    rs_kv = Scatter(dkv_g, dkv_bufs, cores=False)
    rs_kv.first()
    ag_down.finish()
    attn = attn_t[...].T
    out_g[...] = (mm(attn, ag_dense.value(), 1, 1) + mm(act, ag_down.value(), 1, 1)).reshape(out_g.shape)
    z_out = z_scatter(out_g, out_snd, out_rcv)
    down_g[...] = mm(gt_s[...], act).reshape(down_g.shape)
    rs_down = Scatter(down_g, down_bufs)
    dense_g[...] = mm(gt_s[...], attn).reshape(dense_g.shape)
    rs_dense = Scatter(dense_g, dense_bufs)
    rs_kv.second()
    rs_down.first()
    rs_dense.first()
    dpre = mm(g, ag_down.value()) * slope
    dpre_b = dpre.astype(BF)
    up_g[...] = mm(z2t_s[...], dpre_b).reshape(up_g.shape)
    rs_up = Scatter(up_g, up_bufs)
    dz2 = mm(dpre_b, ag_up.value(), 1, 1)
    kv_top, kv_low = rs_kv.finish()
    dkv = jnp.concatenate([kv_top, kv_low], axis=0)
    dq = dq_t[...].T
    parts = []
    for h in range(heads):
        parts += [dq[:, h * HD : (h + 1) * HD], dkv[:, 128 * h : 128 * h + 128]]
    parts.append(jnp.zeros((tok, wide - 3 * hc), F32))
    dproj = turn(jnp.concatenate(parts, axis=1), cos_ref[...], -sina_ref[...], -sinb_ref[...])
    dproj_b = dproj.astype(BF)[:, : 3 * hc]
    dz1 = mm(dproj_b, ag_qkv.value(), 1, 1)
    t_g[...] = (dz1 * gain_ref[0:1, :] + dz2 * gain_ref[1:2, :]).reshape(t_g.shape)
    z_t = z_scatter(t_g, t_snd, t_rcv)
    qkv_g[...] = mm(z1t_s[...], dproj_b).reshape(qkv_g.shape)
    rs_qkv = Scatter(qkv_g, qkv_bufs)
    fin = z_sum(z_out, out_g, out_rcv)
    out_fin[z] = (x_ref[z].astype(F32) + outb_ref[...].reshape(1, -1) + fin).astype(BF)
    c_out = z_gather(out_fin)
    rs_up.first()
    rs_down.second()
    rs_dense.second()
    xhat = xhat_s[...].reshape(tok, feat)
    sm_z[z, 0:1, :] = jnp.sum(dz1 * xhat, axis=0, keepdims=True)
    sm_z[z, 1:2, :] = jnp.sum(dz2 * xhat, axis=0, keepdims=True)
    sm_z[z, 2:3, :] = jnp.sum(dz1, axis=0, keepdims=True)
    sm_z[z, 3:4, :] = jnp.sum(dz2, axis=0, keepdims=True)
    c_sm = z_gather(sm_z)
    rs_qkv.first()
    rs_up.second()
    for cp in c_sm:
        cp.wait_recv()
    me = 4 * c + t
    sm = sm_z[0]
    for i in range(1, tp):
        sm = sm + sm_z[i]
    sm_p[me] = sm
    sm_p[me, 4:5, :] = jnp.sum(g.astype(F32), axis=0, keepdims=True)
    sm_p[me, 5:6, 0 : dpre.shape[1]] = jnp.sum(dpre, axis=0, keepdims=True)
    sm_p[me, 6:7, 0:wide] = jnp.sum(dproj, axis=0, keepdims=True)
    c_pl = [rcopy(sm_p.at[me], sm_p.at[me], dev) for dev in peers]
    tt = z_sum(z_t, t_g, t_rcv)
    xh = xhat_s[z]
    back = inv_s[z, :, 0:1] * (
        tt - jnp.mean(tt, axis=-1, keepdims=True) - xh * jnp.mean(tt * xh, axis=-1, keepdims=True)
    )
    t_fin[z] = (g_ref[z].astype(F32) + back).astype(BF)
    c_t = z_gather(t_fin)
    rs_qkv.second()
    for rs, out in ((rs_dense, dense_out), (rs_down, down_out), (rs_up, up_out), (rs_qkv, qkv_out)):
        top, low = rs.finish()
        out[pl.ds(0, rs.h), :] = top
        out[pl.ds(rs.h, rs.h), :] = low
    for cp in c_pl:
        cp.wait_recv()
    sm = sm_p[0]
    for i in range(1, 8):
        sm = sm + sm_p[i]
    small_out[...] = sm
    for cp in c_out:
        cp.wait_recv()
    layer_out[...] = out_fin[...]
    for cp in c_t:
        cp.wait_recv()
    grad_in[...] = t_fin[...]
    assert len(copies) <= n_copies
    for cp in copies:
        cp.wait_send()


def settle_kernel(heads, lay, gin, small, gqkv, gdense, gup, gdown, *outs):
    o_lay, o_gin, o_gain, o_shift, o_qkv, o_qv, o_dense, o_up, o_upb, o_down, o_outb = outs
    o_lay[...] = lay[...].reshape(o_lay.shape)
    o_gin[...] = gin[...].reshape(o_gin.shape)
    o_gain[...] = small[0:2, :]
    o_shift[...] = small[2:4, :]
    o_qkv[...] = gqkv[...]
    o_dense[...] = gdense[...]
    o_up[...] = gup[...]
    o_down[...] = gdown[...]
    o_outb[...] = small[4:5, :].reshape(o_outb.shape)
    o_upb[...] = small[5:6, 0 : o_upb.shape[0]].reshape(o_upb.shape)
    qv = []
    for h in range(heads):
        qv += [small[6:7, 192 * h : 192 * h + HD], small[6:7, 192 * h + 2 * HD : 192 * h + 192]]
    o_qv[...] = jnp.concatenate(qv, axis=1).reshape(o_qv.shape)


def one_kernel(tp, *args):
    x, span, gains, shifts, wqkv, qvb, wdense, wup, upb, wdown, outb, g = args
    tok, feat = x.shape[1:]
    rows = wqkv.shape[0]
    heads = qvb.shape[0] // (2 * HD)
    ff = wup.shape[1]
    wide = -(-3 * heads * HD // 128) * 128
    piece = tok // tp
    cols = (wqkv.shape[1], wdense.shape[1], ff, ff)
    kvw = 2 * heads * HD

    def bufs(r, w, cores=True):
        h = r // 2
        first = [pltpu.VMEM((4, r, w), BF)] * 2 if cores else [pltpu.VMEM((8, 128), F32)] * 2
        return tuple(first + [pltpu.VMEM((2, h, w), BF)] * 4 + [pltpu.VMEM((h, w), BF)] * 4)

    vm = pltpu.VMEM
    scratch = [vm((8, rows, w), BF) for w in cols]
    scratch += [
        vm((4, tok, kvw), BF),
        vm((tp, piece, feat), F32),
        vm((tp, piece, 128), F32),
        vm((feat, tok), BF),
        vm((feat, tok), BF),
        vm((feat, tok), BF),
        vm((heads * HD, tok), BF),
        vm((heads * HD, tok), F32),
        vm((4, tok, kvw), F32),
        bufs(tok, kvw, False),
    ]
    for w in cols:
        scratch += [vm((8, rows, w), F32), bufs(rows, w)]
    for i in range(2):
        scratch += [
            vm((tp, piece, feat), F32),
            vm((tp, piece, feat), BF),
            vm((tp - 1, piece, feat), BF),
            vm((tp, piece, feat), BF),
        ]
    n_copies = 128
    scratch += [
        vm((tp, 8, feat), F32),
        vm((8, 8, feat), F32),
        vm((tok, wide), F32),
        vm((tok, wide), F32),
        vm((tok, wide), F32),
        pltpu.SemaphoreType.DMA((n_copies,)),
        pltpu.SemaphoreType.DMA((n_copies,)),
    ]
    vspec = pl.BlockSpec(memory_space=pltpu.VMEM)
    specs = [vspec] * 12
    specs[1] = pl.BlockSpec(memory_space=pltpu.SMEM)
    sds = jax.ShapeDtypeStruct
    layer_out, grad_in, small, gqkv, gdense, gup, gdown = pl.pallas_call(
        functools.partial(block_kernel, tp, heads, n_copies),
        out_shape=(
            sds((tp, piece, feat), BF),
            sds((tp, piece, feat), BF),
            sds((8, feat), F32),
        )
        + tuple(sds((rows, w), F32) for w in cols),
        in_specs=specs,
        out_specs=tuple([vspec] * 7),
        scratch_shapes=scratch,
        compiler_params=pltpu.CompilerParams(
            collective_id=0, has_side_effects=True, vmem_limit_bytes=60 * 1024 * 1024
        ),
    )(
        x.reshape(tp, piece, feat),
        span,
        gains,
        shifts,
        wqkv,
        qvb,
        wdense,
        wup,
        upb,
        wdown,
        outb,
        g.reshape(tp, piece, feat),
    )
    pieces = (layer_out, grad_in, small, gqkv, gdense, gup, gdown)
    out = pl.pallas_call(
        functools.partial(settle_kernel, heads),
        out_shape=(
            sds((1, tok, feat), BF),
            sds((1, tok, feat), BF),
            sds((2, feat), F32),
            sds((2, feat), F32),
            sds(gqkv.shape, F32),
            sds((2 * heads * HD,), F32),
            sds(gdense.shape, F32),
            sds(gup.shape, F32),
            sds((ff,), F32),
            sds(gdown.shape, F32),
            sds((feat,), F32),
        ),
        in_specs=[vspec] * 7,
        out_specs=tuple([vspec] * 11),
    )(*pieces)
    return tuple(out)


def solution(mesh):
    placed = (
        P("dp", "ctx", None),
        P("dp", None),
        P(),
        P(),
        P(("dp", "ctx"), "tp"),
        P("tp"),
        P(("dp", "ctx"), "tp"),
        P(("dp", "ctx"), "tp"),
        P("tp"),
        P(("dp", "ctx"), "tp"),
        P(),
        P("dp", "ctx", None),
    )
    sizes = dict(mesh.shape)
    body = on_device
    if sizes["dp"] == 2 and sizes["ctx"] == 4:
        body = functools.partial(one_kernel, sizes["tp"])
    return jax.shard_map(
        body,
        mesh=mesh,
        in_specs=placed,
        out_specs=(
            P("dp", "ctx", None),
            P("dp", "ctx", None),
            P(),
            P(),
            P(("dp", "ctx"), "tp"),
            P("tp"),
            P(("dp", "ctx"), "tp"),
            P(("dp", "ctx"), "tp"),
            P("tp"),
            P(("dp", "ctx"), "tp"),
            P(),
        ),
        check_vma=False,
    )
```

```python
import functools
import math

import jax
import jax.numpy as jnp
from jax import lax
from jax.experimental import pallas as pl
from jax.experimental.pallas import tpu as pltpu
from jax.sharding import PartitionSpec as P

HD = 64
ROT = 16
SPAN = 128


EPS = 1e-05
NEG = -1e30


def layer_norm(values, gain_vec, shift_vec):
    row_mean = jnp.mean(values, axis=-1, keepdims=True)
    centered = values - row_mean
    variance = jnp.mean(centered * centered, axis=-1, keepdims=True)
    inv_std = lax.rsqrt(variance + EPS)
    normed = centered * inv_std
    return (normed * gain_vec + shift_vec, normed, inv_std)


def norm_back(grad_normed, normed, inv_std, gain_vec):
    scaled = grad_normed * gain_vec
    return inv_std * (
        scaled
        - jnp.mean(scaled, axis=-1, keepdims=True)
        - normed * jnp.mean(scaled * normed, axis=-1, keepdims=True)
    )


def rotary_tables(positions, rot_dims):
    half_rot = rot_dims // 2
    frequency = 1.0 / 10000.0 ** (jnp.arange(half_rot, dtype=jnp.float32) * (2.0 / rot_dims))
    angles = positions.astype(jnp.float32)[:, None] * frequency[None, :]
    return (jnp.cos(angles), jnp.sin(angles))


def rotate(vectors, cos_table, sin_table, rot_dims):
    half_rot = rot_dims // 2
    front_half = vectors[..., :half_rot]
    back_half = vectors[..., half_rot:rot_dims]
    cos_row = cos_table[:, None, :]
    sin_row = sin_table[:, None, :]
    return jnp.concatenate(
        [
            front_half * cos_row - back_half * sin_row,
            back_half * cos_row + front_half * sin_row,
            vectors[..., rot_dims:],
        ],
        axis=-1,
    )


def gelu_value(hidden):
    return 0.5 * hidden * (1.0 + jax.scipy.special.erf(hidden * (1.0 / math.sqrt(2.0))))


def gelu_slope(hidden):
    return 0.5 * (1.0 + jax.scipy.special.erf(hidden * (1.0 / math.sqrt(2.0)))) + hidden * jnp.exp(
        -0.5 * hidden * hidden
    ) * (1.0 / math.sqrt(2.0 * math.pi))


def on_device(
    hidden_in,
    span_order,
    norm_gains,
    norm_biases,
    w_qkv,
    qv_bias,
    w_dense,
    w_up,
    up_bias,
    w_down,
    out_bias,
    grad_out,
):
    tok_rows = hidden_in.shape[1]
    local_heads = qv_bias.shape[0] // (2 * HD)
    head_cols = local_heads * HD
    score_scale = 1.0 / math.sqrt(HD)
    positions = (
        span_order[0][:, None] * SPAN + jnp.arange(SPAN, dtype=jnp.int32)[None, :]
    ).reshape(-1)
    own_pos = lax.dynamic_slice_in_dim(positions, lax.axis_index("ctx") * tok_rows, tok_rows)
    full_qkv, full_dense, full_up, full_down = (
        lax.all_gather(w_qkv, ("dp", "ctx"), axis=0, tiled=True),
        lax.all_gather(w_dense, ("dp", "ctx"), axis=0, tiled=True),
        lax.all_gather(w_up, ("dp", "ctx"), axis=0, tiled=True),
        lax.all_gather(w_down, ("dp", "ctx"), axis=0, tiled=True),
    )
    inputs = hidden_in[0].astype(jnp.float32)
    normed_one, hat_one, inv_one = layer_norm(inputs, norm_gains[0], norm_biases[0])
    normed_two, hat_two, inv_two = layer_norm(inputs, norm_gains[1], norm_biases[1])
    attn_in = normed_one.astype(jnp.bfloat16)
    mlp_in = normed_two.astype(jnp.bfloat16)
    projected = jnp.dot(attn_in, full_qkv, preferred_element_type=jnp.float32).reshape(
        tok_rows, local_heads, 3, HD
    )
    bias_pair = qv_bias.reshape(local_heads, 2, HD)
    cos_table, sin_table = rotary_tables(own_pos, ROT)
    queries = rotate(projected[:, :, 0] + bias_pair[:, 0], cos_table, sin_table, ROT).astype(
        jnp.bfloat16
    )
    keys_rot = rotate(projected[:, :, 1], cos_table, sin_table, ROT).astype(jnp.bfloat16)
    values_in = (projected[:, :, 2] + bias_pair[:, 1]).astype(jnp.bfloat16)
    kv_flat = jnp.concatenate(
        [keys_rot.reshape(tok_rows, head_cols), values_in.reshape(tok_rows, head_cols)], axis=-1
    )

    def split_keys(kv_piece):
        piece_rows = kv_piece.shape[0]
        group_rows = math.gcd(piece_rows, 4 * tok_rows)
        block_count = piece_rows // group_rows
        key_pos = positions.reshape(block_count, group_rows)
        key_blocks = kv_piece[:, :head_cols].reshape(block_count, group_rows, local_heads, HD)
        value_blocks = kv_piece[:, head_cols:].reshape(block_count, group_rows, local_heads, HD)
        return (key_blocks, value_blocks, key_pos)

    def key_block(state_in, block_in):
        key_blk, value_blk, key_pos = block_in
        run_max, run_total, run_acc = state_in
        scores = (
            jnp.einsum("qhd,khd->hqk", queries, key_blk, preferred_element_type=jnp.float32)
            * score_scale
        )
        allowed = (key_pos[None, :] <= own_pos[:, None])[None]
        scores = jnp.where(allowed, scores, NEG)
        new_max = jnp.maximum(run_max, jnp.max(scores, axis=-1))
        weights = jnp.where(allowed, jnp.exp(scores - new_max[..., None]), 0.0)
        factor = jnp.exp(run_max - new_max)
        run_total = run_total * factor + jnp.sum(weights, axis=-1)
        run_acc = run_acc * factor[..., None] + jnp.einsum(
            "hqk,khd->hqd",
            weights.astype(jnp.bfloat16),
            value_blk,
            preferred_element_type=jnp.float32,
        )
        return ((new_max, run_total, run_acc), None)

    start_state = (
        jnp.full((local_heads, tok_rows), NEG, jnp.float32),
        jnp.zeros((local_heads, tok_rows), jnp.float32),
        jnp.zeros((local_heads, tok_rows, HD), jnp.float32),
    )
    state_out, unused = lax.scan(
        key_block, start_state, split_keys(lax.all_gather(kv_flat, "ctx", axis=0, tiled=True))
    )
    run_max, run_total, run_acc = state_out
    attn_out = (
        jnp.transpose(run_acc / run_total[..., None], (1, 0, 2))
        .reshape(tok_rows, head_cols)
        .astype(jnp.bfloat16)
    )
    log_total = run_max + jnp.log(run_total)
    attn_part = jnp.einsum("tc,dc->td", attn_out, full_dense, preferred_element_type=jnp.float32)
    hidden_pre = jnp.dot(mlp_in, full_up, preferred_element_type=jnp.float32) + up_bias
    activated = gelu_value(hidden_pre).astype(jnp.bfloat16)
    mlp_part = jnp.einsum("tf,df->td", activated, full_down, preferred_element_type=jnp.float32)
    branches = lax.psum(attn_part + mlp_part, "tp")
    layer_out = (inputs + out_bias + branches).astype(jnp.bfloat16)
    cotangent = grad_out[0]
    cot_float = cotangent.astype(jnp.float32)
    out_bias_grad = jnp.sum(cot_float, axis=0)
    down_grad = jnp.einsum("td,tf->df", cotangent, activated, preferred_element_type=jnp.float32)
    pre_grad = jnp.dot(cotangent, full_down, preferred_element_type=jnp.float32) * gelu_slope(
        hidden_pre
    )
    up_bias_grad = jnp.sum(pre_grad, axis=0)
    pre_grad_b = pre_grad.astype(jnp.bfloat16)
    up_grad = jnp.einsum("td,tf->df", mlp_in, pre_grad_b, preferred_element_type=jnp.float32)
    normed_two_grad = jnp.einsum(
        "tf,df->td", pre_grad_b, full_up, preferred_element_type=jnp.float32
    )
    dense_grad = jnp.einsum("td,tc->dc", cotangent, attn_out, preferred_element_type=jnp.float32)
    out_grad = (
        jnp.dot(cotangent, full_dense, preferred_element_type=jnp.float32)
        .astype(jnp.bfloat16)
        .reshape(tok_rows, local_heads, HD)
    )
    row_delta = jnp.sum(
        out_grad.astype(jnp.float32)
        * attn_out.reshape(tok_rows, local_heads, HD).astype(jnp.float32),
        axis=-1,
    ).T
    back_kv = lax.all_gather(kv_flat, "ctx", axis=0, tiled=True)

    def pair_grads(key_blk, value_blk, key_pos):
        scores = (
            jnp.einsum("qhd,khd->hqk", queries, key_blk, preferred_element_type=jnp.float32)
            * score_scale
        )
        allowed = (key_pos[None, :] <= own_pos[:, None])[None]
        prob_table = jnp.where(
            allowed, jnp.exp(jnp.where(allowed, scores, NEG) - log_total[..., None]), 0.0
        )
        prob_grad = jnp.einsum(
            "qhd,khd->hqk", out_grad, value_blk, preferred_element_type=jnp.float32
        )
        score_grad = (prob_table * (prob_grad - row_delta[..., None])).astype(jnp.bfloat16)
        return (prob_table, score_grad)

    def grad_block(query_acc, block_in):
        key_blk, value_blk, key_pos = block_in
        prob_table, score_grad = pair_grads(key_blk, value_blk, key_pos)
        query_acc = (
            query_acc
            + jnp.einsum("hqk,khd->hqd", score_grad, key_blk, preferred_element_type=jnp.float32)
            * score_scale
        )
        key_part = (
            jnp.einsum("hqk,qhd->khd", score_grad, queries, preferred_element_type=jnp.float32)
            * score_scale
        )
        value_part = jnp.einsum(
            "hqk,qhd->khd",
            prob_table.astype(jnp.bfloat16),
            out_grad,
            preferred_element_type=jnp.float32,
        )
        group_rows = key_blk.shape[0]
        return (
            query_acc,
            jnp.concatenate(
                [
                    key_part.reshape(group_rows, head_cols),
                    value_part.reshape(group_rows, head_cols),
                ],
                axis=-1,
            ),
        )

    query_acc, kv_terms = lax.scan(
        grad_block, jnp.zeros((local_heads, tok_rows, HD), jnp.float32), split_keys(back_kv)
    )
    kv_grads = lax.psum_scatter(
        kv_terms.reshape(back_kv.shape[0], 2 * head_cols), "ctx", scatter_dimension=0, tiled=True
    )
    key_grad = kv_grads[:, :head_cols].reshape(tok_rows, local_heads, HD)
    value_grad = kv_grads[:, head_cols:].reshape(tok_rows, local_heads, HD)
    query_pre = rotate(jnp.transpose(query_acc, (1, 0, 2)), cos_table, -sin_table, ROT)
    key_pre = rotate(key_grad, cos_table, -sin_table, ROT)
    qv_grad = jnp.stack([jnp.sum(query_pre, axis=0), jnp.sum(value_grad, axis=0)], axis=1).reshape(
        -1
    )
    proj_grad = (
        jnp.stack([query_pre, key_pre, value_grad], axis=2)
        .reshape(tok_rows, 3 * head_cols)
        .astype(jnp.bfloat16)
    )
    qkv_grad = jnp.einsum("td,tc->dc", attn_in, proj_grad, preferred_element_type=jnp.float32)
    normed_one_grad = jnp.einsum(
        "tc,dc->td", proj_grad, full_qkv, preferred_element_type=jnp.float32
    )
    full_one, full_two = lax.psum((normed_one_grad, normed_two_grad), "tp")
    gain_part = jnp.stack(
        [jnp.sum(full_one * hat_one, axis=0), jnp.sum(full_two * hat_two, axis=0)]
    )
    bias_part = jnp.stack([jnp.sum(full_one, axis=0), jnp.sum(full_two, axis=0)])
    input_grad = (
        cot_float
        + norm_back(full_one, hat_one, inv_one, norm_gains[0])
        + norm_back(full_two, hat_two, inv_two, norm_gains[1])
    ).astype(jnp.bfloat16)
    gains_total, biases_total, qv_total, up_bias_total, out_bias_total = lax.psum(
        (gain_part, bias_part, qv_grad, up_bias_grad, out_bias_grad), ("dp", "ctx")
    )
    qkv_total, dense_total, up_total, down_total = (
        lax.psum_scatter(qkv_grad, ("dp", "ctx"), scatter_dimension=0, tiled=True),
        lax.psum_scatter(dense_grad, ("dp", "ctx"), scatter_dimension=0, tiled=True),
        lax.psum_scatter(up_grad, ("dp", "ctx"), scatter_dimension=0, tiled=True),
        lax.psum_scatter(down_grad, ("dp", "ctx"), scatter_dimension=0, tiled=True),
    )
    return (
        layer_out[None],
        input_grad[None],
        gains_total,
        biases_total,
        qkv_total,
        qv_total,
        dense_total,
        up_total,
        up_bias_total,
        down_total,
        out_bias_total,
    )


BF = jnp.bfloat16
F32 = jnp.float32


def mm(a, b, ca=1, cb=0):
    return lax.dot_general(a, b, (((ca,), (cb,)), ((), ())), preferred_element_type=F32)


def turn(x, cos_w, sin_a, sin_b):
    width = x.shape[1]
    return x * cos_w + pltpu.roll(x, width - ROT // 2, 1) * sin_a + pltpu.roll(x, ROT // 2, 1) * sin_b


def block_kernel(
    tp,
    heads,
    n_copies,
    x_ref,
    span_ref,
    gain_ref,
    shift_ref,
    wqkv_ref,
    qvb_ref,
    wdense_ref,
    wup_ref,
    upb_ref,
    wdown_ref,
    outb_ref,
    g_ref,
    layer_out,
    grad_in,
    small_out,
    qkv_out,
    dense_out,
    up_out,
    down_out,
    qkv_w,
    dense_w,
    up_w,
    down_w,
    kv_f,
    xhat_s,
    inv_s,
    z1t_s,
    z2t_s,
    gt_s,
    attn_t,
    dq_t,
    dkv_g,
    dkv_bufs,
    qkv_g,
    qkv_bufs,
    dense_g,
    dense_bufs,
    up_g,
    up_bufs,
    down_g,
    down_bufs,
    out_g,
    out_snd,
    out_rcv,
    out_fin,
    t_g,
    t_snd,
    t_rcv,
    t_fin,
    sm_z,
    sm_p,
    cos_ref,
    sina_ref,
    sinb_ref,
    ssem,
    rsem,
):
    c, t, z = lax.axis_index("dp"), lax.axis_index("ctx"), lax.axis_index("tp")
    xi, yi = t % 2, t // 2
    tx, ty, td = t + 1 - 2 * xi, t + 2 - 4 * yi, 3 - t
    to_x, to_y, to_d, to_c = (c, tx, z), (c, ty, z), (c, td, z), (1 - c, t, z)
    tok = x_ref.shape[0] * x_ref.shape[1]
    feat = x_ref.shape[2]
    spans = tok // SPAN
    hc = heads * HD

    barrier = pltpu.get_barrier_semaphore()
    peers = [to_c, to_x, to_y, to_d] + [(1 - c, o, z) for o in (tx, ty, td)]
    z_peers = [(c, t, (z + d) % tp) for d in range(1, tp)]
    for dev in peers + z_peers:
        pl.semaphore_signal(barrier, inc=1, device_id=dev, device_id_type=pl.DeviceIdType.MESH)
    pl.semaphore_wait(barrier, len(peers + z_peers))

    copies = []

    def rcopy(src, dst, dev):
        i = len(copies)
        cp = pltpu.make_async_remote_copy(
            src_ref=src,
            dst_ref=dst,
            send_sem=ssem.at[i],
            recv_sem=rsem.at[i],
            device_id=dev,
            device_id_type=pl.DeviceIdType.MESH,
        )
        cp.start()
        copies.append(cp)
        return cp

    class Gather:
        def __init__(self, own, full, cores=True):
            self.full, self.cores = full, cores
            self.base = 4 * c if cores else 0
            me = self.base + t
            if own is None:
                own = full.at[me]
            else:
                full[me] = own[...]
            self.half = full.shape[1] // 2
            self.cx = rcopy(own, full.at[me], to_x)
            self.cy = rcopy(own, full.at[me], to_y)
            self.cc = [rcopy(own, full.at[me], to_c)] if cores else []

        def relay(self):
            full, h = self.full, self.half
            sx, sy = self.base + tx, self.base + ty
            self.cx.wait_recv()
            a = full.at[sx, pl.ds(0, h)]
            self.d1 = rcopy(a, a, to_y)
            if self.cores:
                self.cc.append(rcopy(full.at[sx], full.at[sx], to_c))
            self.cy.wait_recv()
            b = full.at[sy, pl.ds(h, h)]
            self.d2 = rcopy(b, b, to_x)
            if self.cores:
                self.cc.append(rcopy(full.at[sy], full.at[sy], to_c))

        def finish(self):
            sd = self.base + td
            self.d1.wait_recv()
            self.d2.wait_recv()
            if self.cores:
                self.cc.append(rcopy(self.full.at[sd], self.full.at[sd], to_c))
                for cp in self.cc:
                    cp.wait_recv()

        def value(self):
            s = self.full.shape
            return self.full[...].reshape(s[0] * s[1], s[2])

    class Scatter:
        def __init__(self, total, bufs, cores=True):
            self.g, self.b, self.cores = total, bufs, cores
            self.h = total.shape[1] // 2
            if cores:
                snd, rcv = bufs[:2]
                snd[...] = total[pl.ds(4 * (1 - c), 4)].astype(BF)
                self.cc = rcopy(snd, rcv, to_c)

        def first(self):
            a1, b1, ra1, rb1 = self.b[2:6]
            h = self.h
            if self.cores:
                self.cc.wait_recv()
                self.s = self.g.at[pl.ds(4 * c, 4)]
                self.s[...] = self.s[...] + self.b[1][...].astype(F32)
            else:
                self.s = self.g
            for k in range(2):
                a1[k] = self.s[2 * k + 1 - xi, pl.ds(0, h)].astype(BF)
                b1[k] = self.s[2 * (1 - yi) + k, pl.ds(h, h)].astype(BF)
            self.ca = rcopy(a1, ra1, to_x)
            self.cb = rcopy(b1, rb1, to_y)

        def second(self):
            ra1, rb1, a2, b2, ra2, rb2 = self.b[4:10]
            h = self.h
            self.ca.wait_recv()
            a2[...] = (self.s[2 * (1 - yi) + xi, pl.ds(0, h)] + ra1[1 - yi].astype(F32)).astype(BF)
            self.ca2 = rcopy(a2, ra2, to_y)
            self.cb.wait_recv()
            b2[...] = (self.s[2 * yi + 1 - xi, pl.ds(h, h)] + rb1[1 - xi].astype(F32)).astype(BF)
            self.cb2 = rcopy(b2, rb2, to_x)

        def finish(self):
            ra1, rb1, a2, b2, ra2, rb2 = self.b[4:10]
            h = self.h
            self.ca2.wait_recv()
            top = self.s[t, pl.ds(0, h)] + ra1[yi].astype(F32) + ra2[...].astype(F32)
            self.cb2.wait_recv()
            low = self.s[t, pl.ds(h, h)] + rb1[xi].astype(F32) + rb2[...].astype(F32)
            return top, low

    def z_scatter(total, snd, rcv):
        snd[...] = total[...].astype(BF)
        return [rcopy(snd.at[(z + d) % tp], rcv.at[d - 1], (c, t, (z + d) % tp)) for d in range(1, tp)]

    def z_sum(cps, total, rcv):
        acc = total[z]
        for d in range(1, tp):
            cps[d - 1].wait_recv()
            acc = acc + rcv[d - 1].astype(F32)
        return acc

    def z_gather(fin):
        return [rcopy(fin.at[z], fin.at[z], dev) for dev in z_peers]

    class LineGather:
        def __init__(self, fin):
            self.moves = []
            for side in (1, -1):
                for k in range(tp - 1):
                    src = fin.at[(z - side * k + tp) % tp]
                    i = n_copies + len(guarded)
                    cp = pltpu.make_async_remote_copy(
                        src_ref=src,
                        dst_ref=src,
                        send_sem=ssem.at[i],
                        recv_sem=rsem.at[i],
                        device_id=(c, t, (z + side + tp) % tp),
                        device_id_type=pl.DeviceIdType.MESH,
                    )
                    has = (z - k >= 0) if side == 1 else (z + k < tp)
                    more = (z + 1 < tp) if side == 1 else (z >= 1)
                    gets = (z - k - 1 >= 0) if side == 1 else (z + k + 1 < tp)
                    guarded.append((cp, has & more))
                    self.moves.append((k, cp, has & more, gets))
            self.step(0)

        def step(self, k):
            for hop, cp, sends, gets in self.moves:
                if hop == k - 1:
                    pl.when(gets)(cp.wait_recv)
            for hop, cp, sends, gets in self.moves:
                if hop == k:
                    pl.when(sends)(cp.start)

    guarded = []
    ag_qkv = Gather(wqkv_ref, qkv_w)
    ag_dense = Gather(wdense_ref, dense_w)

    x = x_ref[...].reshape(tok, feat).astype(F32)
    cen = x - jnp.mean(x, axis=-1, keepdims=True)
    inv = lax.rsqrt(jnp.mean(cen * cen, axis=-1, keepdims=True) + EPS)
    xhat = cen * inv
    xhat_s[...] = xhat.reshape(xhat_s.shape)
    inv_s[...] = jnp.broadcast_to(inv, (tok, 128)).reshape(inv_s.shape)
    z1 = (xhat * gain_ref[0:1, :] + shift_ref[0:1, :]).astype(BF)
    z2 = (xhat * gain_ref[1:2, :] + shift_ref[1:2, :]).astype(BF)
    g = g_ref[...].reshape(tok, feat)
    lane = lax.broadcasted_iota(jnp.int32, (1, SPAN), 1)
    row = lax.broadcasted_iota(jnp.int32, (SPAN, 1), 0)
    wide = -(-3 * hc // 128) * 128
    col_pos = jnp.concatenate([span_ref[0, t * spans + i] * SPAN + row for i in range(spans)], axis=0)
    freq = jnp.zeros((1, 128), F32)
    for f in range(ROT // 2):
        step = 1.0 / 10000.0 ** (f * 2.0 / ROT)
        freq = jnp.where(lane % (ROT // 2) == f, step, freq)
    angle = col_pos.astype(F32) * freq
    reps = wide // 128
    cos_w = jnp.concatenate([jnp.cos(angle)] * reps, axis=1)
    sin_w = jnp.concatenate([jnp.sin(angle)] * reps, axis=1)
    col = lax.broadcasted_iota(jnp.int32, (1, wide), 1)
    turned = (col % (3 * HD) < 2 * HD) & (col < 3 * hc)
    lo = turned & (col % HD < ROT // 2)
    hi = turned & (col % HD >= ROT // 2) & (col % HD < ROT)
    cos_ref[...] = jnp.where(lo | hi, cos_w, 1.0)
    sina_ref[...] = jnp.where(lo, -sin_w, 0.0)
    sinb_ref[...] = jnp.where(hi, sin_w, 0.0)
    qvb = qvb_ref[...].reshape(1, 2 * hc)
    bias = []
    for h in range(heads):
        bias += [qvb[:, 128 * h : 128 * h + HD], jnp.zeros((1, HD), F32), qvb[:, 128 * h + HD : 128 * h + 128]]
    bias = jnp.concatenate(bias + [jnp.zeros((1, wide - 3 * hc), F32)], axis=1)
    sm_z[z] = jnp.zeros(sm_z.shape[1:], F32)
    sm_p[4 * c + t] = jnp.zeros(sm_p.shape[1:], F32)

    ag_qkv.relay()
    ag_up = Gather(wup_ref, up_w)
    ag_dense.relay()
    ag_qkv.finish()
    proj = mm(z1, ag_qkv.value())
    proj = jnp.concatenate([proj, jnp.zeros((tok, wide - proj.shape[1]), F32)], axis=1)
    qkv = turn(proj + bias, cos_ref[...], sina_ref[...], sinb_ref[...])
    queries = [(qkv[:, 192 * h : 192 * h + HD].astype(BF) * BF(0.125)) for h in range(heads)]
    kv_f[t] = jnp.concatenate([qkv[:, 192 * h + HD : 192 * h + 192] for h in range(heads)], axis=1).astype(BF)
    ag_kv = Gather(None, kv_f, cores=False)
    ag_dense.finish()
    dattn = mm(g, ag_dense.value()).astype(BF)
    dattn_t = dattn.T
    gt_s[...] = g.T
    ag_kv.relay()
    ag_up.relay()
    ag_down = Gather(wdown_ref, down_w)
    z1t_s[...] = z1.T
    z2t_s[...] = z2.T
    ag_up.finish()
    pre = mm(z2, ag_up.value()) + upb_ref[...].reshape(1, -1)
    phi = 0.5 * (1.0 + lax.erf(pre * (1.0 / math.sqrt(2.0))))
    act = (pre * phi).astype(BF)
    slope = phi + pre * jnp.exp(-0.5 * pre * pre) * (1.0 / math.sqrt(2.0 * math.pi))
    ag_kv.finish()

    own_pos = jnp.concatenate([span_ref[0, t * spans + i] * SPAN + lane for i in range(spans)], axis=1)
    keys = 4 * tok
    masks = jnp.concatenate(
        [row + span_ref[0, i] * SPAN <= own_pos for i in range(keys // SPAN)], axis=0
    )
    for h in range(heads):
        kvh = kv_f[:, :, 128 * h : 128 * h + 128].reshape(keys, 128)
        k, v = kvh[:, :HD], kvh[:, HD:]
        s = jnp.where(masks, mm(k, queries[h], 1, 1), NEG)
        e = jnp.exp(s - jnp.max(s, axis=0, keepdims=True))
        l_inv = 1.0 / jnp.sum(e, axis=0, keepdims=True)
        o_t = (mm(v, e.astype(BF), 0, 0) * l_inv).astype(BF)
        attn_t[h * HD : (h + 1) * HD, :] = o_t
        da_t = dattn_t[h * HD : (h + 1) * HD, :]
        delta = jnp.sum(da_t.astype(F32) * o_t.astype(F32), axis=0, keepdims=True)
        p = e * l_inv
        ds = (p * (mm(v, da_t) - delta)).astype(BF)
        dq_t[h * HD : (h + 1) * HD, :] = mm(k, ds, 0, 0) * 0.125
        dk = mm(ds, queries[h])
        dv = mm(p.astype(BF), dattn[:, h * HD : (h + 1) * HD])
        dkv_g[:, :, 128 * h : 128 * h + 128] = jnp.concatenate([dk, dv], axis=1).reshape(4, tok, 128)
        if h == 0:
            ag_down.relay()
    rs_kv = Scatter(dkv_g, dkv_bufs, cores=False)
    rs_kv.first()
    ag_down.finish()
    attn = attn_t[...].T
    out_g[...] = (mm(attn, ag_dense.value(), 1, 1) + mm(act, ag_down.value(), 1, 1)).reshape(out_g.shape)
    z_out = z_scatter(out_g, out_snd, out_rcv)
    down_g[...] = mm(gt_s[...], act).reshape(down_g.shape)
    rs_down = Scatter(down_g, down_bufs)
    dense_g[...] = mm(gt_s[...], attn).reshape(dense_g.shape)
    rs_dense = Scatter(dense_g, dense_bufs)
    rs_kv.second()
    rs_down.first()
    rs_dense.first()
    dpre = mm(g, ag_down.value()) * slope
    dpre_b = dpre.astype(BF)
    up_g[...] = mm(z2t_s[...], dpre_b).reshape(up_g.shape)
    rs_up = Scatter(up_g, up_bufs)
    dz2 = mm(dpre_b, ag_up.value(), 1, 1)
    kv_top, kv_low = rs_kv.finish()
    dkv = jnp.concatenate([kv_top, kv_low], axis=0)
    dq = dq_t[...].T
    parts = []
    for h in range(heads):
        parts += [dq[:, h * HD : (h + 1) * HD], dkv[:, 128 * h : 128 * h + 128]]
    parts.append(jnp.zeros((tok, wide - 3 * hc), F32))
    dproj = turn(jnp.concatenate(parts, axis=1), cos_ref[...], -sina_ref[...], -sinb_ref[...])
    dproj_b = dproj.astype(BF)[:, : 3 * hc]
    dz1 = mm(dproj_b, ag_qkv.value(), 1, 1)
    t_g[...] = (dz1 * gain_ref[0:1, :] + dz2 * gain_ref[1:2, :]).reshape(t_g.shape)
    z_t = z_scatter(t_g, t_snd, t_rcv)
    qkv_g[...] = mm(z1t_s[...], dproj_b).reshape(qkv_g.shape)
    rs_qkv = Scatter(qkv_g, qkv_bufs)
    fin = z_sum(z_out, out_g, out_rcv)
    out_fin[z] = (x_ref[z].astype(F32) + outb_ref[...].reshape(1, -1) + fin).astype(BF)
    c_out = LineGather(out_fin)
    rs_up.first()
    rs_down.second()
    rs_dense.second()
    xhat = xhat_s[...].reshape(tok, feat)
    sm_z[z, 0:1, :] = jnp.sum(dz1 * xhat, axis=0, keepdims=True)
    sm_z[z, 1:2, :] = jnp.sum(dz2 * xhat, axis=0, keepdims=True)
    sm_z[z, 2:3, :] = jnp.sum(dz1, axis=0, keepdims=True)
    sm_z[z, 3:4, :] = jnp.sum(dz2, axis=0, keepdims=True)
    c_sm = z_gather(sm_z)
    rs_qkv.first()
    c_out.step(1)
    rs_up.second()
    me = 4 * c + t
    for cp in c_sm:
        cp.wait_recv()
    sm = sm_z[0]
    for i in range(1, tp):
        sm = sm + sm_z[i]
    sm_p[me] = sm
    sm_p[me, 4:5, :] = jnp.sum(g.astype(F32), axis=0, keepdims=True)
    sm_p[me, 5:6, 0 : dpre.shape[1]] = jnp.sum(dpre, axis=0, keepdims=True)
    sm_p[me, 6:7, 0:wide] = jnp.sum(dproj, axis=0, keepdims=True)
    c_pl = [rcopy(sm_p.at[me], sm_p.at[me], dev) for dev in peers]
    c_out.step(2)
    tt = z_sum(z_t, t_g, t_rcv)
    xh = xhat_s[z]
    back = inv_s[z, :, 0:1] * (
        tt - jnp.mean(tt, axis=-1, keepdims=True) - xh * jnp.mean(tt * xh, axis=-1, keepdims=True)
    )
    t_fin[z] = (g_ref[z].astype(F32) + back).astype(BF)
    c_t = LineGather(t_fin)
    rs_qkv.second()

    def finish(rs, out):
        top, low = rs.finish()
        out[pl.ds(0, rs.h), :] = top
        out[pl.ds(rs.h, rs.h), :] = low

    finish(rs_dense, dense_out)
    finish(rs_down, down_out)
    c_t.step(1)
    finish(rs_up, up_out)
    for k in range(3, tp):
        c_out.step(k)
    layer_out[...] = out_fin[...]
    for k in range(2, tp - 1):
        c_t.step(k)
    finish(rs_qkv, qkv_out)
    for cp in c_pl:
        cp.wait_recv()
    sm = sm_p[0]
    for i in range(1, 8):
        sm = sm + sm_p[i]
    small_out[...] = sm
    c_t.step(tp - 1)
    grad_in[...] = t_fin[...]
    for cp, sends in guarded:
        pl.when(sends)(cp.wait_send)
    assert len(copies) <= n_copies
    for cp in copies:
        cp.wait_send()


def settle_kernel(heads, lay, gin, small, gqkv, gdense, gup, gdown, *outs):
    o_lay, o_gin, o_gain, o_shift, o_qkv, o_qv, o_dense, o_up, o_upb, o_down, o_outb = outs
    o_lay[...] = lay[...].reshape(o_lay.shape)
    o_gin[...] = gin[...].reshape(o_gin.shape)
    o_gain[...] = small[0:2, :]
    o_shift[...] = small[2:4, :]
    o_qkv[...] = gqkv[...]
    o_dense[...] = gdense[...]
    o_up[...] = gup[...]
    o_down[...] = gdown[...]
    o_outb[...] = small[4:5, :].reshape(o_outb.shape)
    o_upb[...] = small[5:6, 0 : o_upb.shape[0]].reshape(o_upb.shape)
    qv = []
    for h in range(heads):
        qv += [small[6:7, 192 * h : 192 * h + HD], small[6:7, 192 * h + 2 * HD : 192 * h + 192]]
    o_qv[...] = jnp.concatenate(qv, axis=1).reshape(o_qv.shape)


def one_kernel(tp, *args):
    x, span, gains, shifts, wqkv, qvb, wdense, wup, upb, wdown, outb, g = args
    tok, feat = x.shape[1:]
    rows = wqkv.shape[0]
    heads = qvb.shape[0] // (2 * HD)
    ff = wup.shape[1]
    wide = -(-3 * heads * HD // 128) * 128
    piece = tok // tp
    cols = (wqkv.shape[1], wdense.shape[1], ff, ff)
    kvw = 2 * heads * HD

    def bufs(r, w, cores=True):
        h = r // 2
        first = [pltpu.VMEM((4, r, w), BF)] * 2 if cores else [pltpu.VMEM((8, 128), F32)] * 2
        return tuple(first + [pltpu.VMEM((2, h, w), BF)] * 4 + [pltpu.VMEM((h, w), BF)] * 4)

    vm = pltpu.VMEM
    scratch = [vm((8, rows, w), BF) for w in cols]
    scratch += [
        vm((4, tok, kvw), BF),
        vm((tp, piece, feat), F32),
        vm((tp, piece, 128), F32),
        vm((feat, tok), BF),
        vm((feat, tok), BF),
        vm((feat, tok), BF),
        vm((heads * HD, tok), BF),
        vm((heads * HD, tok), F32),
        vm((4, tok, kvw), F32),
        bufs(tok, kvw, False),
    ]
    for w in cols:
        scratch += [vm((8, rows, w), F32), bufs(rows, w)]
    for i in range(2):
        scratch += [
            vm((tp, piece, feat), F32),
            vm((tp, piece, feat), BF),
            vm((tp - 1, piece, feat), BF),
            vm((tp, piece, feat), BF),
        ]
    n_copies = 128
    scratch += [
        vm((tp, 8, feat), F32),
        vm((8, 8, feat), F32),
        vm((tok, wide), F32),
        vm((tok, wide), F32),
        vm((tok, wide), F32),
        pltpu.SemaphoreType.DMA((n_copies + 4 * tp,)),
        pltpu.SemaphoreType.DMA((n_copies + 4 * tp,)),
    ]
    vspec = pl.BlockSpec(memory_space=pltpu.VMEM)
    specs = [vspec] * 12
    specs[1] = pl.BlockSpec(memory_space=pltpu.SMEM)
    sds = jax.ShapeDtypeStruct
    layer_out, grad_in, small, gqkv, gdense, gup, gdown = pl.pallas_call(
        functools.partial(block_kernel, tp, heads, n_copies),
        out_shape=(
            sds((tp, piece, feat), BF),
            sds((tp, piece, feat), BF),
            sds((8, feat), F32),
        )
        + tuple(sds((rows, w), F32) for w in cols),
        in_specs=specs,
        out_specs=tuple([vspec] * 7),
        scratch_shapes=scratch,
        compiler_params=pltpu.CompilerParams(
            collective_id=0, has_side_effects=True, vmem_limit_bytes=60 * 1024 * 1024
        ),
    )(
        x.reshape(tp, piece, feat),
        span,
        gains,
        shifts,
        wqkv,
        qvb,
        wdense,
        wup,
        upb,
        wdown,
        outb,
        g.reshape(tp, piece, feat),
    )
    pieces = (layer_out, grad_in, small, gqkv, gdense, gup, gdown)
    out = pl.pallas_call(
        functools.partial(settle_kernel, heads),
        out_shape=(
            sds((1, tok, feat), BF),
            sds((1, tok, feat), BF),
            sds((2, feat), F32),
            sds((2, feat), F32),
            sds(gqkv.shape, F32),
            sds((2 * heads * HD,), F32),
            sds(gdense.shape, F32),
            sds(gup.shape, F32),
            sds((ff,), F32),
            sds(gdown.shape, F32),
            sds((feat,), F32),
        ),
        in_specs=[vspec] * 7,
        out_specs=tuple([vspec] * 11),
    )(*pieces)
    return tuple(out)


def solution(mesh):
    placed = (
        P("dp", "ctx", None),
        P("dp", None),
        P(),
        P(),
        P(("dp", "ctx"), "tp"),
        P("tp"),
        P(("dp", "ctx"), "tp"),
        P(("dp", "ctx"), "tp"),
        P("tp"),
        P(("dp", "ctx"), "tp"),
        P(),
        P("dp", "ctx", None),
    )
    sizes = dict(mesh.shape)
    body = on_device
    if sizes["dp"] == 2 and sizes["ctx"] == 4:
        body = functools.partial(one_kernel, sizes["tp"])
    return jax.shard_map(
        body,
        mesh=mesh,
        in_specs=placed,
        out_specs=(
            P("dp", "ctx", None),
            P("dp", "ctx", None),
            P(),
            P(),
            P(("dp", "ctx"), "tp"),
            P("tp"),
            P(("dp", "ctx"), "tp"),
            P(("dp", "ctx"), "tp"),
            P("tp"),
            P(("dp", "ctx"), "tp"),
            P(),
        ),
        check_vma=False,
    )
```
